256 devices in a mesh: rcv: 32 (over z, x_hi, core), frq: 8 (over x_lo, y).
Axes of the slice: x: 4 (x_hi: 2, x_lo: 2; x = x_hi * 2 + x_lo), y: 4, z: 8, core: 2. Of those that a mesh axis runs over, the one named last changes fastest.
Arguments:
- spectra: bfloat16 [2, 256, 128, 8192], P(None, None, 'frq', 'rcv'), may hold values from -6 to 6
- virtual_sources: int32 [128], replicated, may hold values from 0 to 8191, as said below
- references: int32 [256], replicated, may hold values from 0 to 8191, as said below
- coda_start: int32 [128], replicated, may hold values from 64 to 255
- coda_end: int32 [128], replicated, may hold values from 384 to 511
Outputs:
- correlations: float32 [2, 128, 256, 8192], P(None, 'frq', None, 'rcv')
The draws below stay inside these ranges and needn't reach their ends.
Inputs may be any that keep to these rules, and one draw needn't show every extreme that they name: `virtual_sources`: distinct receivers; virtual source v is one of the receivers (v // 4) * 256 to (v // 4 + 1) * 256 - 1. `references`: distinct receivers; reference p is one of the receivers (p // 8) * 256 to (p // 8 + 1) * 256 - 1.
All inputs are finite; a program needn't handle non-finite values.
Results may differ from the reference program's by a relative error of at most 0.0068.
Values may be sent and summed in bfloat16 or wider, within the bound.
A program may use at most 64 MiB of HBM per device.

```python
import math
import jax
import jax.numpy as jnp
from jax import lax

R_DEV = 256
W = 256
F = 128
L = 1024
V = 128
P_SIZE = 256
R = 8192
SRC_BLOCK = 4
REF_BLOCK = 8


def blocked_picks(key, count, per_block):
    block_count = R // R_DEV

    def one_block(block_index):
        shuffled = jax.random.permutation(jax.random.fold_in(key, block_index), R_DEV)
        return shuffled[:per_block].astype(jnp.int32) + block_index * R_DEV
    return jax.vmap(one_block)(jnp.arange(block_count, dtype=jnp.int32)).reshape(count)


def draw_virtual_sources(key, part):
    return blocked_picks(jax.random.fold_in(key, 11), V, SRC_BLOCK)


def draw_references(key, part):
    return blocked_picks(jax.random.fold_in(key, 23), P_SIZE, REF_BLOCK)


def with_ends(values, stream_key, smallest, largest):
    index_at = [jax.random.randint(jax.random.fold_in(stream_key, axis), (), 0, length) for axis, length in enumerate(values.shape)]
    widest = values.shape.index(max(values.shape))
    beside = index_at[:widest] + [(index_at[widest] + 1) % values.shape[widest]] + index_at[widest + 1:]
    return values.at[tuple(index_at)].set(smallest).at[tuple(beside)].set(largest)


def levels(stream_key, shape, cuts, low, top_value):
    def one(axis_at, parts):
        steps = jax.random.uniform(jax.random.fold_in(jax.random.fold_in(stream_key, 6), axis_at), (parts,), jnp.float32, low / len(cuts), top_value / len(cuts))
        return jnp.repeat(jnp.exp(steps), shape[axis_at] // parts).reshape((-1,) + (1,) * (len(shape) - axis_at - 1))

    level = one(*cuts[0])
    for cut in cuts[1:]:
        level = level * one(*cut)
    return level


def normal_values(own_key, dims, deviation, limit, cuts=(), held_as=jnp.bfloat16):
    loudness = levels(own_key, dims, cuts, -0.22, 0.18) if cuts else 1.0
    values = jax.random.normal(own_key, dims, jnp.float32) * deviation * loudness
    return jnp.minimum(jnp.maximum(values, -limit), limit).astype(held_as)


def setup_inputs(seed: int = 0) -> dict:
    key_of = jax.random.split(jax.random.key(seed), 6)
    return {
        "spectra": normal_values(key_of[0], (2, W, F, R), 1.0, 6.0, ((2, 8), (3, 32))),
        "virtual_sources": draw_virtual_sources(jax.random.fold_in(key_of[5], 71), 0),
        "references": draw_references(jax.random.fold_in(key_of[5], 71), 0),
        "coda_start": with_ends(jax.random.randint(key_of[3], (V,), L // 16, L // 4), jax.random.fold_in(key_of[3], 1), L // 16, (L // 4) - 1).astype(jnp.int32),
        "coda_end": with_ends(jax.random.randint(key_of[4], (V,), 3 * L // 8, L // 2), jax.random.fold_in(key_of[4], 1), 3 * L // 8, (L // 2) - 1).astype(jnp.int32),
    }


def lag_tables(freq_count, lag_count, first_lag, lag_width):
    lag_values = first_lag + jnp.arange(lag_width, dtype=jnp.int32)
    bin_numbers = jnp.arange(freq_count, dtype=jnp.int32) + 1
    phase_steps = bin_numbers[:, None] * lag_values[None, :] % lag_count
    angles = phase_steps.astype(jnp.float32) * (2.0 * math.pi / lag_count)
    return (jnp.cos(angles), jnp.sin(angles))

def taper_weights(coda_start, coda_end, lag_count):
    lag_values = jnp.arange(lag_count, dtype=jnp.int32)
    lag_reach = jnp.where(lag_values < lag_count // 2, lag_values, lag_count - lag_values)[:, None]
    coda_first = coda_start[None, :]
    coda_last = coda_end[None, :]
    inside = (lag_reach >= coda_first) & (lag_reach < coda_last)
    window_span = (coda_last - coda_first).astype(jnp.float32)
    sine_value = jnp.sin(math.pi * ((lag_reach - coda_first).astype(jnp.float32) + 0.5) / window_span)
    return jnp.where(inside, sine_value * sine_value, jnp.zeros_like(sine_value))

def recompress(spectra_block, taper_table, lag_count):
    freq_count = spectra_block.shape[1]
    src_count = spectra_block.shape[2]
    rcv_count = spectra_block.shape[3]
    flattened = spectra_block.reshape(2 * freq_count, src_count * rcv_count)
    lag_width = min(lag_count, 256)
    accumulated = jnp.zeros((2 * freq_count, src_count * rcv_count), jnp.float32)
    for lag_block in range(lag_count // lag_width):
        first_lag = lag_block * lag_width
        cosine_table, sine_table = lag_tables(freq_count, lag_count, first_lag, lag_width)
        stacked = jnp.concatenate([cosine_table, -sine_table], axis=0)
        inverse = (stacked.T * (1.0 / math.sqrt(freq_count))).astype(jnp.bfloat16)
        forward = (stacked * (4.0 / math.sqrt(lag_count))).astype(jnp.bfloat16)
        series = jnp.dot(inverse, flattened, preferred_element_type=jnp.float32)
        weights = taper_table[first_lag:first_lag + lag_width]
        shaped = series.reshape(lag_width, src_count, rcv_count) * weights[:, :, None]
        squashed = (shaped / jnp.sqrt(1.0 + shaped * shaped)).astype(jnp.bfloat16)
        squashed = squashed.reshape(lag_width, src_count * rcv_count)
        accumulated = accumulated + jnp.dot(forward, squashed, preferred_element_type=jnp.float32)
    return accumulated.astype(jnp.bfloat16).reshape(2, freq_count, src_count, rcv_count)

def cross_spectra(sources, spectra_block, window_count):
    sources = sources.astype(jnp.float32)
    spectra_block = spectra_block.astype(jnp.float32)
    left_side = jnp.concatenate([sources[0], sources[1]], axis=0)
    right_real = jnp.concatenate([spectra_block[0], spectra_block[1]], axis=0)
    right_imag = jnp.concatenate([spectra_block[1], -spectra_block[0]], axis=0)
    real_part = jnp.einsum('wfv,wfr->fvr', left_side, right_real)
    imag_part = jnp.einsum('wfv,wfr->fvr', left_side, right_imag)
    return (jnp.stack([real_part, imag_part]) / math.sqrt(window_count)).astype(jnp.bfloat16)

def recorrelate(picked, relayed, src_total):
    picked = picked.astype(jnp.float32)
    relayed = relayed.astype(jnp.float32)
    left_side = jnp.concatenate([picked[0], picked[1]], axis=1)
    right_real = jnp.concatenate([relayed[0], relayed[1]], axis=1)
    right_imag = jnp.concatenate([relayed[1], -relayed[0]], axis=1)
    real_part = jnp.einsum('fvp,fvr->fpr', left_side, right_real)
    imag_part = jnp.einsum('fvp,fvr->fpr', left_side, right_imag)
    return jnp.stack([real_part, imag_part]) / math.sqrt(src_total)

def reference(spectra, virtual_sources, references, coda_start, coda_end):
    sources = jnp.take(spectra, virtual_sources, axis=3)
    taper_table = taper_weights(coda_start, coda_end, L)
    block_count = R // R_DEV
    blocks = spectra.reshape(2, W, F, block_count, R_DEV).transpose(3, 0, 1, 2, 4)

    def one_block(piece):
        return recompress(cross_spectra(sources, piece, W), taper_table, L)
    relayed_blocks = lax.map(one_block, blocks)
    relayed = relayed_blocks.transpose(1, 2, 3, 0, 4).reshape(2, F, V, R)
    picked = jnp.take(relayed, references, axis=3)
    result_blocks = lax.map(lambda piece: recorrelate(picked, piece, V), relayed_blocks)
    return result_blocks.transpose(1, 2, 3, 0, 4).reshape(2, F, P_SIZE, R)
```

```python
import functools
import math

import jax
import jax.numpy as jnp
import ml_dtypes
import numpy as np
from jax import lax
from jax.experimental import pallas as pl
from jax.experimental.pallas import tpu as pltpu
from jax.sharding import PartitionSpec as P

L = 1024
LAG_FIRST = 64
LAG_HALF = 448
LAGS = 2 * LAG_HALF
NZ, NH, NK = 8, 2, 2
NX, NY = 2, 4
NF = NX * NY
CH = 4
MESH = pl.DeviceIdType.MESH
BF16 = jnp.bfloat16
F32 = jnp.float32


def lag_constants(freq_total, freq_dev):
    reach = LAG_FIRST + np.arange(LAG_HALF, dtype=np.int64)
    lags = np.concatenate([reach, L - reach])
    bins = np.arange(freq_total, dtype=np.int64) + 1
    steps = bins[:, None] * lags[None, :] % L
    angles = steps.astype(np.float32) * np.float32(2.0 * math.pi / L)
    both = np.stack([np.cos(angles), -np.sin(angles)])
    both = both.reshape(2, NF, freq_dev, LAGS).transpose(1, 0, 2, 3).reshape(2 * freq_total, LAGS)
    inverse = (both.T * np.float32(1.0 / math.sqrt(freq_total))).astype(ml_dtypes.bfloat16)
    forward = (both * np.float32(4.0 / math.sqrt(L))).astype(ml_dtypes.bfloat16)
    swap = np.zeros((256, 256), np.float32)
    for a in range(16):
        for b in range(16):
            swap[a * 16 + b, b * 16 + a] = 1.0
    return inverse, forward, swap.astype(ml_dtypes.bfloat16)


def dot(a, b):
    return jnp.dot(a, b, preferred_element_type=F32)


def dot_nt(a, b):
    return lax.dot_general(a, b, (((1,), (1,)), ((), ())), preferred_element_type=F32)


def onehot_rows(idx_ref, first, count, base):
    row = lax.broadcasted_iota(jnp.int32, (16, 256), 0)
    lane = lax.broadcasted_iota(jnp.int32, (16, 256), 1)
    out = jnp.zeros((16, 256), F32)
    for i in range(count):
        hit = (row == i) & (lane == idx_ref[first + i] - base)
        out = jnp.where(hit, 1.0, out)
    return out.astype(BF16)


def c3_kernel(
    vs_ref, rf_ref, cs_ref, ce_ref, inv_ref, fwd_ref, swap_ref, spec_hbm,
    rel_hbm, pick_hbm,
    spec, bank, ag_a, left, mix, send1, recv1, send2, recv2, series, squashed, tap, rel, ag_b,
    load_sem, out_sem,
    a1s, a1r, a2s, a2r, a3s, a3r,
    b1s, b1r, b2s, b2r, b3s, b3r,
    x1s, x1r, x2s, x2r,
):
    mr = lax.axis_index("rcv")
    mf = lax.axis_index("frq")
    mz, mh, mk = mr // 4, (mr // 2) % 2, mr % 2
    mx, my = mf // NY, mf % NY

    def rcv_of(z, h, k):
        return (z * NH + h) * NK + k

    z_peers = [(rcv_of((mz + o) % NZ, mh, mk), mf) for o in range(1, NZ)]
    h_peer = (rcv_of(mz, 1 - mh, mk), mf)
    k_peer = (rcv_of(mz, mh, 1 - mk), mf)
    f_shift = [(dx, dy) for dx in range(NX) for dy in range(NY) if dx or dy]
    f_peers = [((mx + dx) % NX) * NY + (my + dy) % NY for dx, dy in f_shift]

    barrier = pltpu.get_barrier_semaphore()
    peers = z_peers + [h_peer, k_peer] + [(mr, j) for j in f_peers]
    for peer in peers:
        pl.semaphore_signal(barrier, inc=1, device_id=peer, device_id_type=MESH)

    loads = [
        pltpu.make_async_copy(
            spec_hbm.at[pl.ds(i * 128, 128)], spec.at[pl.ds(i * 128, 128)], load_sem.at[i]
        )
        for i in range(4)
    ]
    for load in loads:
        load.start()

    def swapped(block):
        return dot(swap_ref[...], block)

    for i in range(4):
        loads[i].wait()

        def relay(n, _):
            off = pl.multiple_of(n * 16, 16)
            block = spec[pl.ds(off, 16)].reshape(256, 256)
            bank[:, pl.ds(off, 16), :] = swapped(block).astype(BF16).reshape(16, 16, 256)
            return 0

        lax.fori_loop(i * 8, i * 8 + 8, relay, 0)

    pick_v = onehot_rows(vs_ref, mr * 4, 4, mr * 256)

    def select(f, _):
        mix_rows = dot_nt(pick_v, bank[f]).astype(BF16)
        left[f, 0:16, :] = mix_rows
        return 0

    lax.fori_loop(0, 16, select, 0)
    chosen = dot(swap_ref[0:64, :], left[:, 0:16, :].reshape(256, 512)).astype(BF16)
    for c in range(CH):
        ag_a[c, mz, mh, mk] = chosen[c * 16 : c * 16 + 16]

    def remote(src, dst, ssem, rsem, dev):
        return pltpu.make_async_remote_copy(
            src_ref=src, dst_ref=dst, send_sem=ssem, recv_sem=rsem,
            device_id=dev, device_id_type=MESH,
        )

    class Gather:
        def __init__(self, view, sems):
            s1, r1, s2, r2, s3, r3 = sems
            one = view(mz, mh, mk)
            self.first = remote(one, one, s1, r1, h_peer)
            two = view(mz, slice(None), mk)
            self.second = [
                remote(two, two, s2.at[o], r2.at[o], z_peers[o]) for o in range(NZ - 1)
            ]
            half = view(slice(None), slice(None), mk)
            self.third = remote(half, half, s3, r3, k_peer)

        def start2(self):
            self.first.wait_recv()
            for copy in self.second:
                copy.start()

        def start3(self):
            for copy in self.second:
                copy.wait_recv()
            self.third.start()

        def finish(self):
            self.first.wait_send()
            for copy in self.second:
                copy.wait_send()
            self.third.wait_send()

    def gather_a(c):
        return Gather(
            lambda z, h, k: ag_a.at[c, z, h, k],
            (a1s.at[c], a1r.at[c], a2s.at[c], a2r.at[c], a3s.at[c], a3r.at[c]),
        )

    def gather_b(c):
        return Gather(
            lambda z, h, k: ag_b.at[z, h, k, :, pl.ds(c * 1024, 1024)],
            (b1s.at[c], b1r.at[c], b2s.at[c], b2r.at[c], b3s.at[c], b3r.at[c]),
        )

    ga = [gather_a(c) for c in range(CH)]
    gb = [gather_b(c) for c in range(CH)]

    pl.semaphore_wait(barrier, len(peers))
    for c in range(CH):
        ga[c].first.start()
    ga[0].start2()

    reach = LAG_FIRST + lax.broadcasted_iota(jnp.int32, (LAG_HALF, 128), 0)
    first, last = cs_ref[...], ce_ref[...]
    inside = (reach >= first) & (reach < last)
    span = (last - first).astype(F32)
    sine = jnp.sin(math.pi * ((reach - first).astype(F32) + 0.5) / span)
    weights = jnp.where(inside, sine * sine, 0.0)
    weights = pltpu.roll(weights, (128 - 16 * mf) % 128, 1)
    for v in range(16):
        tap[v] = jnp.broadcast_to(weights[:, v : v + 1], (LAG_HALF, 128))

    def exchange(c, src, dst, ssem, rsem):
        return [
            remote(src(c, f_peers[i]), dst(c, mf), ssem.at[c, i], rsem.at[c, i], (mr, f_peers[i]))
            for i in range(NF - 1)
        ]

    def rows(j):
        return pl.ds(pl.multiple_of(j * 32, 32), 32)

    def quad(j):
        return pl.ds(pl.multiple_of(j * 4, 4), 4)

    ex1 = [
        exchange(
            c,
            lambda c, j: send1.at[c, quad(j)],
            lambda c, j: recv1.at[c, :, rows(j), :],
            x1s, x1r,
        )
        for c in range(CH)
    ]
    ex2 = [
        exchange(
            c,
            lambda c, j: send2.at[c, :, rows(j), :],
            lambda c, j: recv2.at[c, quad(j)],
            x2s, x2r,
        )
        for c in range(CH)
    ]

    def cross_step(c):
        for g in range(2):
            block = swapped(ag_a[c, g * 4 : g * 4 + 4].reshape(256, 512))
            plain = block.astype(BF16).reshape(16, 16, 512)
            minus = (-block).astype(BF16).reshape(16, 16, 512)
            left[:, g * 16 : g * 16 + 16, :] = plain
            left[:, 32 + g * 16 : 48 + g * 16, 0:256] = minus[:, :, 256:512]
            left[:, 32 + g * 16 : 48 + g * 16, 256:512] = plain[:, :, 0:256]

        def one_bin(f, _):
            out = (dot(left[f], bank[f]) * 0.0625).astype(BF16)
            off = pl.multiple_of(f * 16, 16)
            mix[:, pl.ds(off, 16), :] = out.reshape(4, 16, 256)
            return 0

        lax.fori_loop(0, 16, one_bin, 0)
        for part in range(2):
            for g in range(2):
                block = swapped(mix[part * 2 + g]).astype(BF16)
                send1[c, g * 16 : g * 16 + 16, part * 16 : part * 16 + 16, :] = block.reshape(
                    16, 16, 256
                )
        for copy in ex1[c]:
            copy.start()
        recv1[c, :, rows(mf), :] = send1[c, quad(mf)]

    def lag_step(c):
        for copy in ex1[c]:
            copy.wait_recv()

        def one_source(q, _):
            series[...] = dot(inv_ref[...], recv1[c, q])
            for n in range(7):
                w = tap[q * 4 + c, n * 64 : n * 64 + 64, :]
                w = jnp.concatenate([w, w], axis=1)
                for h in range(2):
                    at = h * LAG_HALF + n * 64
                    x = series[at : at + 64, :] * w
                    squashed[at : at + 64, :] = (x * lax.rsqrt(1.0 + x * x)).astype(BF16)
            send2[c, q] = dot(fwd_ref[...], squashed[...]).astype(BF16)
            return 0

        lax.fori_loop(0, 4, one_source, 0)
        for copy in ex2[c]:
            copy.start()
        recv2[c, quad(mf)] = send2[c, :, rows(mf), :]

    pick_p = onehot_rows(rf_ref, mr * 8, 8, mr * 256)
    outs = []

    def turn_step(c):
        for copy in ex2[c]:
            copy.wait_recv()
        for part in range(2):
            for g in range(2):
                block = recv2[c, g * 16 : g * 16 + 16, part * 16 : part * 16 + 16, :]
                block = swapped(block.reshape(256, 256)).astype(BF16).reshape(16, 16, 256)
                at = c * 64 + part * 32 + g * 16
                rel[:, at : at + 16, :] = block
        out = pltpu.make_async_copy(
            rel.at[:, pl.ds(c * 64, 64), :], rel_hbm.at[:, pl.ds(c * 64, 64), :], out_sem.at[c]
        )
        out.start()
        outs.append(out)
        for n in range(4):
            block = rel[n * 4 : n * 4 + 4, c * 64 : c * 64 + 64, :].reshape(256, 256)
            got = dot_nt(pick_p, block)[0:8].astype(BF16)
            ag_b[mz, mh, mk, :, c * 1024 + n * 256 : c * 1024 + n * 256 + 256] = got
        gb[c].first.start()

    def head(c):
        ga[c].start3()
        if c + 1 < CH:
            ga[c + 1].start2()
        ga[c].third.wait_recv()
        cross_step(c)

    def land(c):
        gb[c].third.wait_recv()
        out = pltpu.make_async_copy(
            ag_b.at[:, :, :, :, pl.ds(c * 1024, 1024)],
            pick_hbm.at[:, :, :, :, pl.ds(c * 1024, 1024)],
            out_sem.at[CH + c],
        )
        out.start()
        outs.append(out)

    head(0)
    head(1)
    lag_step(0)
    head(2)
    lag_step(1)
    head(3)
    lag_step(2)
    turn_step(0)
    lag_step(3)
    gb[0].start2()
    turn_step(1)
    gb[0].start3()
    gb[1].start2()
    turn_step(2)
    land(0)
    gb[1].start3()
    gb[2].start2()
    turn_step(3)
    land(1)
    gb[2].start3()
    gb[3].start2()
    land(2)
    gb[3].start3()
    land(3)

    for c in range(CH):
        ga[c].finish()
        gb[c].finish()
        for copy in ex1[c] + ex2[c]:
            copy.wait_send()
    for out in outs:
        out.wait()


def final_kernel(scale, p0, p1, p2, p3, rel_ref, out_ref, right):
    @pl.when(pl.program_id(0) == 0)
    def _():
        right[...] = jnp.zeros_like(right)

    lhs = jnp.concatenate([p0[...], p1[...], p2[...], p3[...]], axis=1)
    for b in range(2):
        for c in range(CH):
            real = rel_ref[b, c * 64 : c * 64 + 32, :]
            imag = rel_ref[b, c * 64 + 32 : c * 64 + 64, :]
            at = c * 128 + b * 64
            right[b, at : at + 32, 0:256] = real
            right[b, at + 32 : at + 64, 0:256] = imag
            right[b, at : at + 32, 256:512] = imag
            right[b, at + 32 : at + 64, 256:512] = -real
        out = dot(lhs, right[b]) * scale
        out_ref[0, b] = out[:, 0:256]
        out_ref[1, b] = out[:, 256:512]


def per_device(spectra, virtual_sources, references, coda_start, coda_end):
    windows, freq_dev, rcv_dev = spectra.shape[1:]
    sources = virtual_sources.shape[0]
    picks = references.shape[0]
    inverse, forward, swap = lag_constants(freq_dev * NF, freq_dev)
    vmem = pl.BlockSpec(memory_space=pltpu.VMEM)
    smem = pl.BlockSpec(memory_space=pltpu.SMEM)
    hbm = pl.BlockSpec(memory_space=pl.ANY)
    dma = pltpu.SemaphoreType.DMA
    gather_sems = [dma((CH,))] * 2 + [dma((CH, NZ - 1))] * 2 + [dma((CH,))] * 2
    rel, picked = pl.pallas_call(
        c3_kernel,
        out_shape=(
            jax.ShapeDtypeStruct((16, 256, 256), BF16),
            jax.ShapeDtypeStruct((NZ, NH, NK, 8, 4096), BF16),
        ),
        in_specs=[smem, smem, vmem, vmem, vmem, vmem, vmem, hbm],
        out_specs=(hbm, hbm),
        scratch_shapes=[
            pltpu.VMEM((512, 16, 256), BF16),
            pltpu.VMEM((16, 512, 256), BF16),
            pltpu.VMEM((CH, NZ, NH, NK, 16, 512), BF16),
            pltpu.VMEM((16, 64, 512), BF16),
            pltpu.VMEM((4, 256, 256), BF16),
            pltpu.VMEM((CH, 32, 32, 256), BF16),
            pltpu.VMEM((CH, 4, 256, 256), BF16),
            pltpu.VMEM((CH, 4, 256, 256), BF16),
            pltpu.VMEM((CH, 32, 32, 256), BF16),
            pltpu.VMEM((LAGS, 256), F32),
            pltpu.VMEM((LAGS, 256), BF16),
            pltpu.VMEM((16, LAG_HALF, 128), F32),
            pltpu.VMEM((16, 256, 256), BF16),
            pltpu.VMEM((NZ, NH, NK, 8, 4096), BF16),
            dma((4,)),
            dma((2 * CH,)),
        ]
        + gather_sems
        + gather_sems
        + [dma((CH, NF - 1))] * 4,
        compiler_params=pltpu.CompilerParams(
            collective_id=0, has_side_effects=True, vmem_limit_bytes=56 << 20
        ),
        name="c3_exchange",
    )(
        virtual_sources,
        references,
        coda_start.reshape(1, sources),
        coda_end.reshape(1, sources),
        jnp.asarray(inverse),
        jnp.asarray(forward),
        jnp.asarray(swap),
        spectra.reshape(2 * windows, freq_dev, rcv_dev),
    )
    picked = picked.reshape(picks, 4096)
    lane_block = lambda c: pl.BlockSpec((256, 128), lambda n: (0, c * 8 + n))
    return pl.pallas_call(
        functools.partial(final_kernel, 1.0 / math.sqrt(sources)),
        grid=(8,),
        out_shape=jax.ShapeDtypeStruct((2, freq_dev, picks, rcv_dev), F32),
        in_specs=[lane_block(c) for c in range(CH)]
        + [pl.BlockSpec((2, 256, 256), lambda n: (n, 0, 0))],
        out_specs=pl.BlockSpec((2, 2, 256, 256), lambda n: (0, n, 0, 0)),
        scratch_shapes=[pltpu.VMEM((2, 512, 512), BF16)],
        compiler_params=pltpu.CompilerParams(vmem_limit_bytes=32 << 20),
        name="recorrelate",
    )(picked, picked, picked, picked, rel)


def solution(mesh):
    return jax.shard_map(
        per_device,
        mesh=mesh,
        in_specs=(P(None, None, "frq", "rcv"), P(), P(), P(), P()),
        out_specs=P(None, "frq", None, "rcv"),
        check_vma=False,
    )
```

```python
import functools
import math

import jax
import jax.numpy as jnp
import ml_dtypes
import numpy as np
from jax import lax
from jax.experimental import pallas as pl
from jax.experimental.pallas import tpu as pltpu
from jax.sharding import PartitionSpec as P

L = 1024
LAG_FIRST = 64
LAG_HALF = 448
LAGS = 2 * LAG_HALF
NZ, NH, NK = 8, 2, 2
NX, NY = 2, 4
NF = NX * NY
FINAL_BINS = 8
CH = 4
DEPTH = 8
MESH = pl.DeviceIdType.MESH
BF16 = jnp.bfloat16
F32 = jnp.float32


def lag_constants(freq_total, freq_dev):
    reach = LAG_FIRST + np.arange(LAG_HALF, dtype=np.int64)
    lags = np.concatenate([reach, L - reach])
    bins = np.arange(freq_total, dtype=np.int64) + 1
    steps = bins[:, None] * lags[None, :] % L
    angles = steps.astype(np.float32) * np.float32(2.0 * math.pi / L)
    both = np.stack([np.cos(angles), -np.sin(angles)])
    both = both.reshape(2, NF, 2, freq_dev // 2, LAGS).transpose(1, 2, 0, 3, 4)
    both = both.reshape(2 * freq_total, LAGS)
    inverse = (both.T * np.float32(1.0 / math.sqrt(freq_total))).astype(ml_dtypes.bfloat16)
    forward = (both * np.float32(4.0 / math.sqrt(L))).astype(ml_dtypes.bfloat16)
    swap = np.zeros((256, 256), np.float32)
    for a in range(16):
        for b in range(16):
            swap[a * 16 + b, b * 16 + a] = 1.0
    piece = np.zeros((128, 512), np.float32)
    for v in range(4):
        for f in range(16):
            for part in range(2):
                piece[(v * 16 + f) * 2 + part, part * 256 + f * 16 + v] = 1.0
    return inverse, forward, swap.astype(ml_dtypes.bfloat16), piece.astype(ml_dtypes.bfloat16)


def dot(a, b):
    return jnp.dot(a, b, preferred_element_type=F32)


def dot_nt(a, b):
    return lax.dot_general(a, b, (((1,), (1,)), ((), ())), preferred_element_type=F32)


def onehot_rows(idx_ref, first, count, base):
    row = lax.broadcasted_iota(jnp.int32, (16, 256), 0)
    lane = lax.broadcasted_iota(jnp.int32, (16, 256), 1)
    out = jnp.zeros((16, 256), F32)
    for i in range(count):
        hit = (row == i) & (lane == idx_ref[first + i] - base)
        out = jnp.where(hit, 1.0, out)
    return out.astype(BF16)


def c3_kernel(
    vs_ref, rf_ref, cs_ref, ce_ref, inv_hbm, fwd_hbm, swap_ref, piece_ref, spec_hbm,
    rel_hbm, pick_hbm,
    spec, bank, ag_a, left, mix, send1, recv1, send2, recv2, series, squashed, tap, rel, ag_b,
    inv_ref, fwd_ref, load_sem, out_sem,
    a1s, a1r, a2s, a2r, a3s, a3r,
    d1s, d1r, d2s, d2r,
    x1s, x1r, x2s, x2r,
):
    mr = lax.axis_index("rcv")
    mf = lax.axis_index("frq")
    mz, mh, mk = mr // 4, (mr // 2) % 2, mr % 2
    mx, my = mf // NY, mf % NY

    def rcv_of(z, h, k):
        return (z * NH + h) * NK + k

    plane_peers = [
        (rcv_of((mz + o) % NZ, (mh + p) % NH, mk), mf)
        for p in range(NH)
        for o in (4, 3, 5, 2, 6, 1, 7, 0)
        if o or p
    ]
    h_peer = (rcv_of(mz, 1 - mh, mk), mf)
    k_peer = (rcv_of(mz, mh, 1 - mk), mf)
    f_shift = [(dx, dy) for dx in range(NX) for dy in range(NY) if dx or dy]
    f_peers = [((mx + dx) % NX) * NY + (my + dy) % NY for dx, dy in f_shift]

    barrier = pltpu.get_barrier_semaphore()
    peers = plane_peers + [k_peer] + [(mr, j) for j in f_peers]
    for peer in peers:
        pl.semaphore_signal(barrier, inc=1, device_id=peer, device_id_type=MESH)

    loads = [
        pltpu.make_async_copy(
            spec_hbm.at[pl.ds(i * 64, 64)], spec.at[pl.ds(i * 64, 64)], load_sem.at[i]
        )
        for i in range(8)
    ]
    tables = [
        pltpu.make_async_copy(inv_hbm, inv_ref, load_sem.at[8]),
        pltpu.make_async_copy(fwd_hbm, fwd_ref, load_sem.at[9]),
    ]
    for load in loads + tables:
        load.start()

    def swapped(block):
        return dot(swap_ref[...], block)

    for i in range(8):
        loads[i].wait()

        def relay(n, _):
            off = pl.multiple_of(n * 16, 16)
            block = spec[pl.ds(off, 16)].reshape(256, 256)
            bank[:, pl.ds(off, 16), :] = swapped(block).astype(BF16).reshape(16, 16, 256)
            return 0

        lax.fori_loop(i * 4, i * 4 + 4, relay, 0, unroll=4)

    pick_v = onehot_rows(vs_ref, mr * 4, 4, mr * 256)

    def select(f, _):
        mix_rows = dot_nt(pick_v, bank[f]).astype(BF16)
        left[f, 0:16, :] = mix_rows
        return 0

    lax.fori_loop(0, 16, select, 0, unroll=4)
    chosen = jnp.concatenate(
        [left[:, 0:16, 0:256].reshape(256, 256), left[:, 0:16, 256:512].reshape(256, 256)], axis=0
    )
    chosen = dot(piece_ref[...], chosen).astype(BF16)
    for c in range(CH):
        for half in range(2):
            at = c * 32 + half * 16
            ag_a[c, half, mz, mh, mk] = chosen[at : at + 16]

    def remote(src, dst, ssem, rsem, dev):
        return pltpu.make_async_remote_copy(
            src_ref=src, dst_ref=dst, send_sem=ssem, recv_sem=rsem,
            device_id=dev, device_id_type=MESH,
        )

    def z_peer(o):
        return rcv_of((mz + o) % NZ, mh, mk), mf

    class Gather:
        def __init__(self, view, sems):
            s1, r1, s2, r2, s3, r3 = sems
            one = view(mz, mh, mk)
            self.first = remote(one, one, s1, r1, h_peer)
            two = view(mz, slice(None), mk)
            self.near = [
                remote(two, two, s2.at[i], r2.at[i], z_peer(o))
                for i, o in enumerate((2, -2, 1, -1))
            ]
            self.far = []
            for i, o in enumerate((1, -1)):
                two = view((mz - 2 * o) % NZ, slice(None), mk)
                one = view((mz - 2 * o) % NZ, i, mk)
                self.far.append(
                    [
                        remote(two, two, s2.at[4 + i], r2.at[4 + i], z_peer(o)),
                        remote(one, one, s2.at[6 + i], r2.at[6 + i], z_peer(2 * o)),
                    ]
                )
            half = view(slice(None), slice(None), mk)
            self.third = remote(half, half, s3, r3, k_peer)

        def start1(self):
            self.first.wait_recv()
            for copy in self.near:
                copy.start()

        def start2(self):
            for i in range(2):
                self.near[i].wait_recv()
                for copy in self.far[i]:
                    copy.start()

        def start3(self):
            for copy in self.near[2:] + self.far[0] + self.far[1]:
                copy.wait_recv()
            self.third.start()

        def finish(self):
            self.first.wait_send()
            for copy in self.near + self.far[0] + self.far[1]:
                copy.wait_send()
            self.third.wait_send()

    class Direct:
        def __init__(self, view, sems, out_view=None, out_sem=None):
            s1, r1, s3, r3 = sems
            one = view(mz, mh, mk)
            self.near = [
                remote(one, one, s1.at[i], r1.at[i], peer) for i, peer in enumerate(plane_peers)
            ]
            half = view(slice(None), slice(None), mk)
            landing = half if out_view is None else out_view(slice(None), slice(None), mk)
            self.third = remote(half, landing, s3, r3, k_peer)
            self.local = None
            if out_view is not None:
                self.local = pltpu.make_async_copy(half, landing, out_sem)

        def start1(self):
            for copy in self.near:
                copy.start()

        def start3(self):
            for copy in self.near:
                copy.wait_recv()
            self.third.start()
            if self.local is not None:
                self.local.start()

        def finish(self):
            for copy in self.near:
                copy.wait_send()
            self.third.wait_send()
            if self.local is not None:
                self.third.wait_recv()
                self.local.wait()

    def pair_sems(c, s1, r1, s2, r2, s3, r3):
        return s1.at[c], r1.at[c], s2.at[c], r2.at[c], s3.at[c], r3.at[c]

    da = [
        Direct(
            lambda z, h, k, half=half: ag_a.at[0, half, z, h, k],
            (d1s.at[half], d1r.at[half], d2s.at[half], d2r.at[half]),
        )
        for half in range(2)
    ]
    ga = [None] + [
        Gather(
            lambda z, h, k, c=c: ag_a.at[c, :, z, h, k],
            pair_sems(c - 1, a1s, a1r, a2s, a2r, a3s, a3r),
        )
        for c in range(1, CH)
    ]
    def pick_gather(n, first, count):
        return Direct(
            lambda z, h, k: ag_b.at[z, h, k, :, pl.ds(first, count)],
            (d1s.at[2 + n], d1r.at[2 + n], d2s.at[2 + n], d2r.at[2 + n]),
            lambda z, h, k: pick_hbm.at[z, h, k, :, pl.ds(first, count)],
            out_sem.at[2, n],
        )

    db = [pick_gather(c, c * 1024, 1024) for c in range(CH - 1)]
    db = db + [pick_gather(CH - 1 + half, 3072 + half * 512, 512) for half in range(2)]

    pl.semaphore_wait(barrier, len(peers))
    da[0].start1()
    for c in range(1, CH):
        ga[c].first.start()

    reach = LAG_FIRST + lax.broadcasted_iota(jnp.int32, (LAG_HALF, 128), 0)
    first, last = cs_ref[...], ce_ref[...]
    inside = (reach >= first) & (reach < last)
    span = (last - first).astype(F32)
    sine = jnp.sin(math.pi * ((reach - first).astype(F32) + 0.5) / span)
    weights = jnp.where(inside, sine * sine, 0.0)
    weights = pltpu.roll(weights, (128 - 16 * mf) % 128, 1)
    for v in range(16):
        tap[v] = jnp.broadcast_to(weights[:, v : v + 1], (LAG_HALF, 128))
    da[1].start1()

    def rows(j):
        return pl.ds(pl.multiple_of(j * 32, 32), 32)

    def part_rows(j, half):
        return pl.ds(pl.multiple_of(j * 32 + half * 16, 16), 16)

    def quad(j):
        return pl.ds(pl.multiple_of(j * 4, 4), 4)

    def exchange(n, src, dst, ssem, rsem):
        return [
            remote(src(j), dst(mf), ssem.at[n, i], rsem.at[n, i], (mr, j))
            for i, j in enumerate(f_peers)
        ]

    ex1 = [
        exchange(
            half,
            lambda j, half=half: send1.at[0, quad(j), pl.ds(half * 16, 16), :],
            lambda j, half=half: recv1.at[0, :, part_rows(j, half), :],
            x1s, x1r,
        )
        for half in range(2)
    ] + [
        exchange(
            c + 1,
            lambda j, c=c: send1.at[c, quad(j)],
            lambda j, c=c: recv1.at[c, :, rows(j), :],
            x1s, x1r,
        )
        for c in range(1, CH)
    ]
    ex2 = [
        exchange(
            c,
            lambda j, c=c: send2.at[c, :, rows(j), :],
            lambda j, c=c: recv2.at[c, quad(j)],
            x2s, x2r,
        )
        for c in range(CH - 1)
    ] + [
        exchange(
            3 + half,
            lambda j, half=half: send2.at[3, :, part_rows(j, half), :],
            lambda j, half=half: recv2.at[3, quad(j), pl.ds(half * 16, 16), :],
            x2s, x2r,
        )
        for half in range(2)
    ]
    issued = []

    def send(group):
        if len(issued) >= DEPTH:
            for copy in issued[-DEPTH]:
                copy.wait_send()
        for copy in group:
            copy.start()
        issued.append(group)

    def cross_half(c, half):
        first = half * 8
        for g in range(2):
            block = swapped(ag_a[c, half, g * 4 : g * 4 + 4].reshape(256, 256))
            plain = block.astype(BF16).reshape(8, 2, 16, 256)
            minus = (-block).astype(BF16).reshape(8, 2, 16, 256)
            at = g * 16
            left[first : first + 8, at : at + 16, 0:256] = plain[:, 0]
            left[first : first + 8, at : at + 16, 256:512] = plain[:, 1]
            left[first : first + 8, 32 + at : 48 + at, 0:256] = minus[:, 1]
            left[first : first + 8, 32 + at : 48 + at, 256:512] = plain[:, 0]

        def one_bin(f, _):
            out = (dot(left[first + f], bank[first + f]) * 0.0625).astype(BF16)
            out = out.reshape(4, 16, 256)
            for part in range(2):
                off = pl.multiple_of(part * 128 + f * 16, 16)
                mix[half, :, pl.ds(off, 16), :] = out[part * 2 : part * 2 + 2]
            return 0

        lax.fori_loop(0, 8, one_bin, 0, unroll=4)
        for g in range(2):
            block = swapped(mix[half, g]).astype(BF16)
            send1[c, g * 16 : g * 16 + 16, half * 16 : half * 16 + 16, :] = block.reshape(
                16, 16, 256
            )

    def cross_first(half):
        da[half].third.wait_recv()
        cross_half(0, half)
        send(ex1[half])
        recv1[0, :, part_rows(mf, half), :] = send1[0, quad(mf), half * 16 : half * 16 + 16, :]

    def cross(c):
        ga[c].third.wait_recv()
        cross_half(c, 0)
        cross_half(c, 1)
        send(ex1[c + 1])
        recv1[c, :, rows(mf), :] = send1[c, quad(mf)]

    def lag_step(c):
        for copy in ex1[0] + ex1[1] if c == 0 else ex1[c + 1]:
            copy.wait_recv()

        def two_sources(pair, _):
            for i in range(2):
                q = pair * 2 + i
                series[i] = dot(inv_ref[...], recv1[c, q])
                for n in range(7):
                    w = tap[q * 4 + c, n * 64 : n * 64 + 64, :]
                    w = jnp.concatenate([w, w], axis=1)
                    for h in range(2):
                        at = h * LAG_HALF + n * 64
                        x = series[i, at : at + 64, :] * w
                        squashed[i, at : at + 64, :] = (x * lax.rsqrt(1.0 + x * x)).astype(BF16)
                send2[c, q] = dot(fwd_ref[...], squashed[i]).astype(BF16)
            return 0

        lax.fori_loop(0, 2, two_sources, 0)
        send(ex2[c])
        if c == CH - 1:
            send(ex2[CH])
        recv2[c, quad(mf)] = send2[c, :, rows(mf), :]

    pick_p = onehot_rows(rf_ref, mr * 8, 8, mr * 256)
    outs = []

    def turn_half(c, half):
        first = half * 8
        for g in range(2):
            block = recv2[c, g * 16 : g * 16 + 16, half * 16 : half * 16 + 16, :]
            block = swapped(block.reshape(256, 256)).astype(BF16).reshape(2, 8, 16, 256)
            for part in range(2):
                at = c * 64 + part * 32 + g * 16
                rel[first : first + 8, at : at + 16, :] = block[part]
        out = pltpu.make_async_copy(
            rel.at[pl.ds(first, 8), pl.ds(c * 64, 64), :],
            rel_hbm.at[pl.ds(first, 8), pl.ds(c * 64, 64), :],
            out_sem.at[half, c],
        )
        out.start()
        outs.append(out)
        for n in range(half * 2, half * 2 + 2):
            order = (1, 0, 3, 2) if c % 2 else (0, 1, 2, 3)
            block = [rel[n * 4 + i, c * 64 : c * 64 + 64, :] for i in order]
            block = jnp.concatenate(block, axis=0)
            got = dot_nt(pick_p, block)[0:8].astype(BF16)
            ag_b[mz, mh, mk, :, c * 1024 + n * 256 : c * 1024 + n * 256 + 256] = got

    def turn_step(c):
        for copy in ex2[c]:
            copy.wait_recv()
        turn_half(c, 0)
        turn_half(c, 1)
        db[c].start1()

    def turn_last(half):
        for copy in ex2[CH - 1 + half]:
            copy.wait_recv()
        turn_half(CH - 1, half)
        db[CH - 1 + half].start1()

    da[0].start3()
    ga[1].start1()
    da[1].start3()
    cross_first(0)
    ga[1].start2()
    ga[2].start1()
    cross_first(1)
    ga[1].start3()
    ga[2].start2()
    ga[3].start1()
    cross(1)
    ga[2].start3()
    ga[3].start2()
    cross(2)
    ga[3].start3()
    for table in tables:
        table.wait()
    lag_step(0)
    cross(3)
    lag_step(1)
    lag_step(2)
    turn_step(0)
    lag_step(3)
    turn_step(1)
    turn_step(2)
    db[0].start3()
    turn_last(0)
    db[1].start3()
    turn_last(1)
    db[2].start3()
    db[3].start3()
    db[4].start3()

    for gather in ga[1:] + da + db:
        gather.finish()
    for group in issued[-DEPTH:]:
        for copy in group:
            copy.wait_send()
    for out in outs:
        out.wait()


def final_kernel(scale, p0, p1, p2, p3, rel_ref, out_ref):
    low = lax.broadcasted_iota(jnp.int32, (256, 128), 1) < 64
    for b in range(FINAL_BINS):
        odd = b % 2
        lanes = slice(b // 2 * 128, b // 2 * 128 + 128)
        pieces = [p[:, lanes] for p in (p0, p1, p2, p3)]
        left, real, imag = [], [], []
        for c in range(CH):
            if c % 2 == 0:
                left.append(jnp.where(low, pieces[c + odd], pieces[c + 1 - odd]))
            at = (c ^ odd) * 64
            one, other = rel_ref[b, at : at + 32, :], rel_ref[b, at + 32 : at + 64, :]
            real += [one, other]
            imag += [other, -one]
        left = jnp.concatenate(left, axis=1)
        out_ref[0, b] = dot(left, jnp.concatenate(real, axis=0)) * scale
        out_ref[1, b] = dot(left, jnp.concatenate(imag, axis=0)) * scale


def per_device(spectra, virtual_sources, references, coda_start, coda_end):
    windows, freq_dev, rcv_dev = spectra.shape[1:]
    sources = virtual_sources.shape[0]
    picks = references.shape[0]
    inverse, forward, swap, piece = lag_constants(freq_dev * NF, freq_dev)
    vmem = pl.BlockSpec(memory_space=pltpu.VMEM)
    smem = pl.BlockSpec(memory_space=pltpu.SMEM)
    hbm = pl.BlockSpec(memory_space=pl.ANY)
    dma = pltpu.SemaphoreType.DMA
    gather_sems = [dma((CH - 1,))] * 2 + [dma((CH - 1, 8))] * 2 + [dma((CH - 1,))] * 2
    rel, picked = pl.pallas_call(
        c3_kernel,
        out_shape=(
            jax.ShapeDtypeStruct((16, 256, 256), BF16),
            jax.ShapeDtypeStruct((NZ, NH, NK, 8, 4096), BF16),
        ),
        in_specs=[smem, smem, vmem, vmem, hbm, hbm, vmem, vmem, hbm],
        out_specs=(hbm, hbm),
        scratch_shapes=[
            pltpu.VMEM((512, 16, 256), BF16),
            pltpu.VMEM((16, 512, 256), BF16),
            pltpu.VMEM((CH, 2, NZ, NH, NK, 16, 256), BF16),
            pltpu.VMEM((16, 64, 512), BF16),
            pltpu.VMEM((2, 2, 256, 256), BF16),
            pltpu.VMEM((CH, 32, 32, 256), BF16),
            pltpu.VMEM((CH, 4, 256, 256), BF16),
            pltpu.VMEM((CH, 4, 256, 256), BF16),
            pltpu.VMEM((CH, 32, 32, 256), BF16),
            pltpu.VMEM((2, LAGS, 256), F32),
            pltpu.VMEM((2, LAGS, 256), BF16),
            pltpu.VMEM((16, LAG_HALF, 128), F32),
            pltpu.VMEM((16, 256, 256), BF16),
            pltpu.VMEM((NZ, NH, NK, 8, 4096), BF16),
            pltpu.VMEM((LAGS, 256), BF16),
            pltpu.VMEM((256, LAGS), BF16),
            dma((10,)),
            dma((3, CH + 1)),
        ]
        + gather_sems
        + [dma((CH + 3, 15))] * 2
        + [dma((CH + 3,))] * 2
        + [dma((CH + 1, NF - 1))] * 4,
        compiler_params=pltpu.CompilerParams(
            collective_id=0, has_side_effects=True, vmem_limit_bytes=56 << 20
        ),
        name="c3_exchange",
    )(
        virtual_sources,
        references,
        coda_start.reshape(1, sources),
        coda_end.reshape(1, sources),
        jnp.asarray(inverse),
        jnp.asarray(forward),
        jnp.asarray(swap),
        jnp.asarray(piece),
        spectra.reshape(2 * windows, freq_dev, rcv_dev),
    )
    picked = picked.reshape(picks, 4096)
    steps = freq_dev // FINAL_BINS
    lane_block = lambda c: pl.BlockSpec(
        (256, 64 * FINAL_BINS), lambda n: (0, c * steps + n)
    )
    return pl.pallas_call(
        functools.partial(final_kernel, 1.0 / math.sqrt(sources)),
        grid=(steps,),
        out_shape=jax.ShapeDtypeStruct((2, freq_dev, picks, rcv_dev), F32),
        in_specs=[lane_block(c) for c in range(CH)]
        + [pl.BlockSpec((FINAL_BINS, 256, 256), lambda n: (n, 0, 0))],
        out_specs=pl.BlockSpec((2, FINAL_BINS, 256, 256), lambda n: (0, n, 0, 0)),
        compiler_params=pltpu.CompilerParams(vmem_limit_bytes=60 << 20),
        name="recorrelate",
    )(picked, picked, picked, picked, rel)


def solution(mesh):
    return jax.shard_map(
        per_device,
        mesh=mesh,
        in_specs=(P(None, None, "frq", "rcv"), P(), P(), P(), P()),
        out_specs=P(None, "frq", None, "rcv"),
        check_vma=False,
    )
```

```python
import functools
import math

import jax
import jax.numpy as jnp
import ml_dtypes
import numpy as np
from jax import lax
from jax.experimental import pallas as pl
from jax.experimental.pallas import tpu as pltpu
from jax.sharding import PartitionSpec as P

L = 1024
LAG_FIRST = 64
LAG_HALF = 448
LAGS = 2 * LAG_HALF
NZ, NH, NK = 8, 2, 2
NX, NY = 2, 4
NF = NX * NY
FINAL_BINS = 8
CH = 4
MESH = pl.DeviceIdType.MESH
BF16 = jnp.bfloat16
F32 = jnp.float32


def lag_constants(freq_total, freq_dev):
    reach = LAG_FIRST + np.arange(LAG_HALF, dtype=np.int64)
    lags = np.concatenate([reach, L - reach])
    bins = np.arange(freq_total, dtype=np.int64) + 1
    steps = bins[:, None] * lags[None, :] % L
    angles = steps.astype(np.float32) * np.float32(2.0 * math.pi / L)
    both = np.stack([np.cos(angles), -np.sin(angles)])
    both = both.reshape(2, NF, 2, freq_dev // 2, LAGS).transpose(1, 2, 0, 3, 4)
    both = both.reshape(2 * freq_total, LAGS)
    inverse = (both.T * np.float32(1.0 / math.sqrt(freq_total))).astype(ml_dtypes.bfloat16)
    forward = (both * np.float32(4.0 / math.sqrt(L))).astype(ml_dtypes.bfloat16)
    swap = np.zeros((256, 256), np.float32)
    for a in range(16):
        for b in range(16):
            swap[a * 16 + b, b * 16 + a] = 1.0
    piece = np.zeros((128, 512), np.float32)
    for v in range(4):
        for f in range(16):
            for part in range(2):
                piece[(v * 16 + f) * 2 + part, part * 256 + f * 16 + v] = 1.0
    return inverse, forward, swap.astype(ml_dtypes.bfloat16), piece.astype(ml_dtypes.bfloat16)


def dot(a, b):
    return jnp.dot(a, b, preferred_element_type=F32)


def dot_nt(a, b):
    return lax.dot_general(a, b, (((1,), (1,)), ((), ())), preferred_element_type=F32)


def onehot_rows(idx_ref, first, count, base):
    row = lax.broadcasted_iota(jnp.int32, (16, 256), 0)
    lane = lax.broadcasted_iota(jnp.int32, (16, 256), 1)
    out = jnp.zeros((16, 256), F32)
    for i in range(count):
        hit = (row == i) & (lane == idx_ref[first + i] - base)
        out = jnp.where(hit, 1.0, out)
    return out.astype(BF16)


def c3_kernel(
    vs_ref, rf_ref, cs_ref, ce_ref, inv_hbm, fwd_hbm, swap_hbm, piece_hbm, spec_hbm,
    rel_hbm, pick_hbm,
    spec, bank, ag_a, left, mix, send1, recv1, send2, recv2, series, squashed, tap, rel, ag_b,
    inv_ref, fwd_ref, swap_ref, piece_ref, load_sem, out_sem,
    a1s, a1r, a2s, a2r, a3s, a3r,
    d0s, d0r, d1s, d1r, d2s, d2r,
    x1s, x1r, x2s, x2r,
):
    mr = lax.axis_index("rcv")
    mf = lax.axis_index("frq")
    mz, mh, mk = mr // 4, (mr // 2) % 2, mr % 2
    mx, my = mf // NY, mf % NY

    def rcv_of(z, h, k):
        return (z * NH + h) * NK + k

    z_peers = [(rcv_of((mz + o) % NZ, mh, mk), mf) for o in range(1, NZ)]
    h_peer = (rcv_of(mz, 1 - mh, mk), mf)
    k_peer = (rcv_of(mz, mh, 1 - mk), mf)
    f_shift = [(dx, dy) for dx in range(NX) for dy in range(NY) if dx or dy]
    f_peers = [((mx + dx) % NX) * NY + (my + dy) % NY for dx, dy in f_shift]

    barrier = pltpu.get_barrier_semaphore()
    peers = z_peers + [h_peer, k_peer] + [(mr, j) for j in f_peers]
    for peer in peers:
        pl.semaphore_signal(barrier, inc=1, device_id=peer, device_id_type=MESH)

    loads = [
        pltpu.make_async_copy(
            spec_hbm.at[pl.ds(i * 64, 64)], spec.at[pl.ds(i * 64, 64)], load_sem.at[i]
        )
        for i in range(8)
    ]
    tables = [
        pltpu.make_async_copy(inv_hbm, inv_ref, load_sem.at[8]),
        pltpu.make_async_copy(fwd_hbm, fwd_ref, load_sem.at[9]),
    ]
    early = [
        pltpu.make_async_copy(swap_hbm, swap_ref, load_sem.at[10]),
        pltpu.make_async_copy(piece_hbm, piece_ref, load_sem.at[11]),
    ]
    for load in early + loads + tables:
        load.start()
    for load in early:
        load.wait()

    def swapped(block):
        return dot(swap_ref[...], block)

    for i in range(8):
        loads[i].wait()

        def relay(n, _):
            off = pl.multiple_of(n * 16, 16)
            block = spec[pl.ds(off, 16)].reshape(256, 256)
            bank[:, pl.ds(off, 16), :] = swapped(block).astype(BF16).reshape(16, 16, 256)
            return 0

        lax.fori_loop(i * 4, i * 4 + 4, relay, 0, unroll=4)

    pick_v = onehot_rows(vs_ref, mr * 4, 4, mr * 256)

    def select(f, _):
        mix_rows = dot_nt(pick_v, bank[f]).astype(BF16)
        left[f, 0:16, :] = mix_rows
        return 0

    lax.fori_loop(0, 16, select, 0, unroll=4)
    chosen = jnp.concatenate(
        [left[:, 0:16, 0:256].reshape(256, 256), left[:, 0:16, 256:512].reshape(256, 256)], axis=0
    )
    chosen = dot(piece_ref[...], chosen).astype(BF16)
    for c in range(CH):
        for half in range(2):
            at = c * 32 + half * 16
            ag_a[c, half, mz, mh, mk] = chosen[at : at + 16]

    def remote(src, dst, ssem, rsem, dev):
        return pltpu.make_async_remote_copy(
            src_ref=src, dst_ref=dst, send_sem=ssem, recv_sem=rsem,
            device_id=dev, device_id_type=MESH,
        )

    def z_peer(o):
        return rcv_of((mz + o) % NZ, mh, mk), mf

    class Group:
        def __init__(self, copies, whole, ssem, rsem):
            self.copies = copies
            self.whole = whole
            self.ssem = ssem
            self.rsem = rsem

        def start(self):
            for copy in self.copies:
                copy.start()

        def wait_send(self):
            pltpu.make_async_copy(self.whole, self.whole, self.ssem).wait()

        def wait_recv(self):
            pltpu.make_async_copy(self.whole, self.whole, self.rsem).wait()

    class Gather:
        def __init__(self, view, sems):
            s1, r1, s2, r2, s3, r3 = sems
            one = view(mz, mh, mk)
            self.first = remote(one, one, s1, r1, h_peer)
            two = view(mz, slice(None), mk)
            self.near = [
                remote(two, two, s2, r2.at[min(i, 2)], z_peer(o))
                for i, o in enumerate((2, -2, 1, -1))
            ]
            self.far = []
            for i, o in enumerate((1, -1)):
                two = view((mz - 2 * o) % NZ, slice(None), mk)
                one = view((mz - 2 * o) % NZ, i, mk)
                self.far.append(
                    [
                        remote(two, two, s2, r2.at[2], z_peer(o)),
                        remote(one, one, s2, r2.at[2], z_peer(2 * o)),
                    ]
                )
            self.all_sent = Group([], view(pl.ds(0, 7), slice(None), mk), s2, s2)
            self.rest = Group([], view(pl.ds(0, 5), slice(None), mk), s2, r2.at[2])
            half = view(slice(None), slice(None), mk)
            self.third = remote(half, half, s3, r3, k_peer)

        def start1(self):
            self.first.wait_recv()
            for copy in self.near:
                copy.start()

        def start2(self):
            for i in range(2):
                self.near[i].wait_recv()
                for copy in self.far[i]:
                    copy.start()

        def start3(self):
            self.rest.wait_recv()
            self.third.start()

        def finish(self):
            self.first.wait_send()
            self.all_sent.wait_send()
            self.third.wait_send()

    class Direct:
        def __init__(self, view, sems, out_view=None, out_sem=None):
            s0, r0, s1, r1, s3, r3 = sems
            one = view(mz, mh, mk)
            self.first = remote(one, one, s0, r0, h_peer)
            two = view(mz, slice(None), mk)
            copies = [remote(two, two, s1, r1, z_peer(o)) for o in (4, 3, 5, 2, 6, 1, 7)]
            self.near = Group(copies, view(pl.ds(0, NZ - 1), slice(None), mk), s1, r1)
            half = view(slice(None), slice(None), mk)
            landing = half if out_view is None else out_view(slice(None), slice(None), mk)
            self.third = remote(half, landing, s3, r3, k_peer)
            self.local = None
            if out_view is not None:
                self.local = pltpu.make_async_copy(half, landing, out_sem)

        def start1(self):
            self.first.wait_recv()
            self.near.start()

        def start3(self):
            self.near.wait_recv()
            self.third.start()
            if self.local is not None:
                self.local.start()

        def finish(self):
            self.first.wait_send()
            self.near.wait_send()
            self.third.wait_send()
            if self.local is not None:
                self.third.wait_recv()
                self.local.wait()

    def pair_sems(c, s1, r1, s2, r2, s3, r3):
        return s1.at[c], r1.at[c], s2.at[c], r2.at[c], s3.at[c], r3.at[c]

    def direct_sems(n):
        return d0s.at[n], d0r.at[n], d1s.at[n], d1r.at[n], d2s.at[n], d2r.at[n]

    da = [
        Direct(
            lambda z, h, k, half=half: ag_a.at[0, half, z, h, k],
            direct_sems(half),
        )
        for half in range(2)
    ]
    ga = [None] + [
        Gather(
            lambda z, h, k, c=c: ag_a.at[c, :, z, h, k],
            pair_sems(c - 1, a1s, a1r, a2s, a2r, a3s, a3r),
        )
        for c in range(1, CH)
    ]
    def pick_gather(n, first, count):
        return Direct(
            lambda z, h, k: ag_b.at[z, h, k, :, pl.ds(first, count)],
            direct_sems(2 + n),
            lambda z, h, k: pick_hbm.at[z, h, k, :, pl.ds(first, count)],
            out_sem.at[2, n],
        )

    db = [pick_gather(c, c * 1024, 1024) for c in range(CH - 1)]
    db = db + [pick_gather(CH - 1 + half, 3072 + half * 512, 512) for half in range(2)]

    pl.semaphore_wait(barrier, len(peers))
    for gather in da + ga[1:]:
        gather.first.start()
    da[0].start1()

    reach = LAG_FIRST + lax.broadcasted_iota(jnp.int32, (LAG_HALF, 128), 0)
    first, last = cs_ref[...], ce_ref[...]
    inside = (reach >= first) & (reach < last)
    span = (last - first).astype(F32)
    sine = jnp.sin(math.pi * ((reach - first).astype(F32) + 0.5) / span)
    weights = jnp.where(inside, sine * sine, 0.0)
    weights = pltpu.roll(weights, (128 - 16 * mf) % 128, 1)
    for v in range(16):
        tap[v] = jnp.broadcast_to(weights[:, v : v + 1], (LAG_HALF, 128))
    da[1].start1()

    def rows(j):
        return pl.ds(pl.multiple_of(j * 32, 32), 32)

    def part_rows(j, half):
        return pl.ds(pl.multiple_of(j * 32 + half * 16, 16), 16)

    def quad(j):
        return pl.ds(pl.multiple_of(j * 4, 4), 4)

    def exchange(n, src, dst, whole, ssem, rsem):
        copies = [remote(src(j), dst(mf), ssem.at[n], rsem.at[n], (mr, j)) for j in f_peers]
        return [Group(copies, whole, ssem.at[n], rsem.at[n])]

    whole_half = send1.at[0, pl.ds(0, 4 * (NF - 1)), pl.ds(0, 16), :]
    whole_full = send1.at[0, pl.ds(0, 4 * (NF - 1))]

    ex1 = [
        exchange(
            half,
            lambda j, half=half: send1.at[0, quad(j), pl.ds(half * 16, 16), :],
            lambda j, half=half: recv1.at[0, :, part_rows(j, half), :],
            whole_half, x1s, x1r,
        )
        for half in range(2)
    ] + [
        exchange(
            c + 1,
            lambda j, c=c: send1.at[c, quad(j)],
            lambda j, c=c: recv1.at[c, :, rows(j), :],
            whole_full, x1s, x1r,
        )
        for c in range(1, CH)
    ]
    ex2 = [
        [
            exchange(
                2 * c + half,
                lambda j, c=c, half=half: send2.at[c, :, part_rows(j, half), :],
                lambda j, c=c, half=half: recv2.at[c, quad(j), pl.ds(half * 16, 16), :],
                whole_half, x2s, x2r,
            )
            for half in range(2)
        ]
        for c in range(CH)
    ]

    def send(group):
        for copy in group:
            copy.start()

    def sent(group):
        for copy in group:
            copy.wait_send()

    def give_back(c, half):
        send(ex2[c][half])

    def cross_half(c, half):
        first = half * 8
        for g in range(2):
            block = swapped(ag_a[c, half, g * 4 : g * 4 + 4].reshape(256, 256))
            plain = block.astype(BF16).reshape(8, 2, 16, 256)
            minus = (-block).astype(BF16).reshape(8, 2, 16, 256)
            at = g * 16
            left[first : first + 8, at : at + 16, 0:256] = plain[:, 0]
            left[first : first + 8, at : at + 16, 256:512] = plain[:, 1]
            left[first : first + 8, 32 + at : 48 + at, 0:256] = minus[:, 1]
            left[first : first + 8, 32 + at : 48 + at, 256:512] = plain[:, 0]

        def one_bin(f, _):
            out = (dot(left[first + f], bank[first + f]) * 0.0625).astype(BF16)
            out = out.reshape(4, 16, 256)
            for part in range(2):
                off = pl.multiple_of(part * 128 + f * 16, 16)
                mix[half, :, pl.ds(off, 16), :] = out[part * 2 : part * 2 + 2]
            return 0

        lax.fori_loop(0, 8, one_bin, 0, unroll=4)
        for g in range(2):
            block = swapped(mix[half, g]).astype(BF16)
            send1[c, g * 16 : g * 16 + 16, half * 16 : half * 16 + 16, :] = block.reshape(
                16, 16, 256
            )

    def cross_first(half):
        da[half].third.wait_recv()
        cross_half(0, half)
        send(ex1[half])
        recv1[0, :, part_rows(mf, half), :] = send1[0, quad(mf), half * 16 : half * 16 + 16, :]

    def cross(c):
        ga[c].third.wait_recv()
        cross_half(c, 0)
        cross_half(c, 1)
        send(ex1[c + 1])
        recv1[c, :, rows(mf), :] = send1[c, quad(mf)]

    def lag_step(c):
        for copy in ex1[0] + ex1[1] if c == 0 else ex1[c + 1]:
            copy.wait_recv()

        def two_sources(pair, _):
            for i in range(2):
                q = pair * 2 + i
                series[i] = dot(inv_ref[...], recv1[c, q])
                for n in range(7):
                    w = tap[q * 4 + c, n * 64 : n * 64 + 64, :]
                    w = jnp.concatenate([w, w], axis=1)
                    for h in range(2):
                        at = h * LAG_HALF + n * 64
                        x = series[i, at : at + 64, :] * w
                        squashed[i, at : at + 64, :] = (x * lax.rsqrt(1.0 + x * x)).astype(BF16)
                send2[c, q] = dot(fwd_ref[...], squashed[i]).astype(BF16)
            return 0

        lax.fori_loop(0, 2, two_sources, 0)
        recv2[c, quad(mf)] = send2[c, :, rows(mf), :]

    pick_p = onehot_rows(rf_ref, mr * 8, 8, mr * 256)
    outs = []

    def turn_half(c, half):
        first = half * 8
        for g in range(2):
            block = recv2[c, g * 16 : g * 16 + 16, half * 16 : half * 16 + 16, :]
            block = swapped(block.reshape(256, 256)).astype(BF16).reshape(2, 8, 16, 256)
            for part in range(2):
                at = c * 64 + part * 32 + g * 16
                rel[first : first + 8, at : at + 16, :] = block[part]
        out = pltpu.make_async_copy(
            rel.at[pl.ds(first, 8), pl.ds(c * 64, 64), :],
            rel_hbm.at[pl.ds(first, 8), pl.ds(c * 64, 64), :],
            out_sem.at[half, c],
        )
        out.start()
        outs.append(out)
        for n in range(half * 2, half * 2 + 2):
            order = (1, 0, 3, 2) if c % 2 else (0, 1, 2, 3)
            block = [rel[n * 4 + i, c * 64 : c * 64 + 64, :] for i in order]
            block = jnp.concatenate(block, axis=0)
            got = dot_nt(pick_p, block)[0:8].astype(BF16)
            ag_b[mz, mh, mk, :, c * 1024 + n * 256 : c * 1024 + n * 256 + 256] = got

    def turn_step(c):
        for copy in ex2[c][0] + ex2[c][1]:
            copy.wait_recv()
        turn_half(c, 0)
        turn_half(c, 1)
        db[c].first.start()

    def turn_last(half):
        for copy in ex2[CH - 1][half]:
            copy.wait_recv()
        turn_half(CH - 1, half)
        db[CH - 1 + half].first.start()

    da[0].start3()
    ga[1].start1()
    cross_first(0)
    da[1].start3()
    ga[1].start2()
    ga[2].start1()
    cross_first(1)
    ga[1].start3()
    ga[2].start2()
    ga[3].start1()
    cross(1)
    ga[2].start3()
    ga[3].start2()
    cross(2)
    ga[3].start3()
    for table in tables:
        table.wait()
    lag_step(0)
    give_back(0, 0)
    give_back(0, 1)
    cross(3)
    lag_step(1)
    give_back(1, 0)
    for gather in da + ga[1:]:
        gather.finish()
    sent(ex1[0] + ex1[1] + ex1[2] + ex1[3])
    turn_step(0)
    give_back(1, 1)
    lag_step(2)
    give_back(2, 0)
    sent(ex1[4] + ex2[0][0] + ex2[0][1])
    db[0].start1()
    turn_step(1)
    give_back(2, 1)
    lag_step(3)
    give_back(3, 0)
    db[1].start1()
    db[0].start3()
    turn_step(2)
    give_back(3, 1)
    sent(ex2[1][0] + ex2[1][1])
    db[0].finish()
    db[2].start1()
    turn_last(0)
    db[1].start3()
    turn_last(1)
    db[3].start1()
    db[4].start1()
    sent(ex2[2][0] + ex2[2][1])
    db[1].finish()
    db[2].start3()
    db[3].start3()
    db[4].start3()

    for c in range(2, CH + 1):
        db[c].finish()
    sent(ex2[3][0] + ex2[3][1])
    for out in outs:
        out.wait()


def final_kernel(scale, p0, p1, p2, p3, rel_ref, out_ref):
    low = lax.broadcasted_iota(jnp.int32, (256, 128), 1) < 64
    for b in range(FINAL_BINS):
        odd = b % 2
        lanes = slice(b // 2 * 128, b // 2 * 128 + 128)
        pieces = [p[:, lanes] for p in (p0, p1, p2, p3)]
        left, real, imag = [], [], []
        for c in range(CH):
            if c % 2 == 0:
                left.append(jnp.where(low, pieces[c + odd], pieces[c + 1 - odd]))
            at = (c ^ odd) * 64
            one, other = rel_ref[b, at : at + 32, :], rel_ref[b, at + 32 : at + 64, :]
            real += [one, other]
            imag += [other, -one]
        left = jnp.concatenate(left, axis=1)
        out_ref[0, b] = dot(left, jnp.concatenate(real, axis=0)) * scale
        out_ref[1, b] = dot(left, jnp.concatenate(imag, axis=0)) * scale


def per_device(spectra, virtual_sources, references, coda_start, coda_end):
    windows, freq_dev, rcv_dev = spectra.shape[1:]
    sources = virtual_sources.shape[0]
    picks = references.shape[0]
    inverse, forward, swap, piece = lag_constants(freq_dev * NF, freq_dev)
    vmem = pl.BlockSpec(memory_space=pltpu.VMEM)
    smem = pl.BlockSpec(memory_space=pltpu.SMEM)
    hbm = pl.BlockSpec(memory_space=pl.ANY)
    dma = pltpu.SemaphoreType.DMA
    gather_sems = [dma((CH - 1,))] * 3 + [dma((CH - 1, 3))] + [dma((CH - 1,))] * 2
    rel, picked = pl.pallas_call(
        c3_kernel,
        out_shape=(
            jax.ShapeDtypeStruct((16, 256, 256), BF16),
            jax.ShapeDtypeStruct((NZ, NH, NK, 8, 4096), BF16),
        ),
        in_specs=[smem, smem, vmem, vmem, hbm, hbm, hbm, hbm, hbm],
        out_specs=(hbm, hbm),
        scratch_shapes=[
            pltpu.VMEM((512, 16, 256), BF16),
            pltpu.VMEM((16, 512, 256), BF16),
            pltpu.VMEM((CH, 2, NZ, NH, NK, 16, 256), BF16),
            pltpu.VMEM((16, 64, 512), BF16),
            pltpu.VMEM((2, 2, 256, 256), BF16),
            pltpu.VMEM((CH, 32, 32, 256), BF16),
            pltpu.VMEM((CH, 4, 256, 256), BF16),
            pltpu.VMEM((CH, 4, 256, 256), BF16),
            pltpu.VMEM((CH, 32, 32, 256), BF16),
            pltpu.VMEM((2, LAGS, 256), F32),
            pltpu.VMEM((2, LAGS, 256), BF16),
            pltpu.VMEM((16, LAG_HALF, 128), F32),
            pltpu.VMEM((16, 256, 256), BF16),
            pltpu.VMEM((NZ, NH, NK, 8, 4096), BF16),
            pltpu.VMEM((LAGS, 256), BF16),
            pltpu.VMEM((256, LAGS), BF16),
            pltpu.VMEM((256, 256), BF16),
            pltpu.VMEM((128, 512), BF16),
            dma((12,)),
            dma((3, CH + 1)),
        ]
        + gather_sems
        + [dma((CH + 3,))] * 2
        + [dma((CH + 3,))] * 2
        + [dma((CH + 3,))] * 2
        + [dma((CH + 1,))] * 2
        + [dma((2 * CH,))] * 2,
        compiler_params=pltpu.CompilerParams(
            collective_id=0, has_side_effects=True, vmem_limit_bytes=56 << 20
        ),
        name="c3_exchange",
    )(
        virtual_sources,
        references,
        coda_start.reshape(1, sources),
        coda_end.reshape(1, sources),
        jnp.asarray(inverse),
        jnp.asarray(forward),
        jnp.asarray(swap),
        jnp.asarray(piece),
        spectra.reshape(2 * windows, freq_dev, rcv_dev),
    )
    picked = picked.reshape(picks, 4096)
    steps = freq_dev // FINAL_BINS
    lane_block = lambda c: pl.BlockSpec(
        (256, 64 * FINAL_BINS), lambda n: (0, c * steps + n)
    )
    return pl.pallas_call(
        functools.partial(final_kernel, 1.0 / math.sqrt(sources)),
        grid=(steps,),
        out_shape=jax.ShapeDtypeStruct((2, freq_dev, picks, rcv_dev), F32),
        in_specs=[lane_block(c) for c in range(CH)]
        + [pl.BlockSpec((FINAL_BINS, 256, 256), lambda n: (n, 0, 0))],
        out_specs=pl.BlockSpec((2, FINAL_BINS, 256, 256), lambda n: (0, n, 0, 0)),
        compiler_params=pltpu.CompilerParams(vmem_limit_bytes=60 << 20),
        name="recorrelate",
    )(picked, picked, picked, picked, rel)


def solution(mesh):
    return jax.shard_map(
        per_device,
        mesh=mesh,
        in_specs=(P(None, None, "frq", "rcv"), P(), P(), P(), P()),
        out_specs=P(None, "frq", None, "rcv"),
        check_vma=False,
    )
```

```python
import functools
import math

import jax
import jax.numpy as jnp
import ml_dtypes
import numpy as np
from jax import lax
from jax.experimental import pallas as pl
from jax.experimental.pallas import tpu as pltpu
from jax.sharding import PartitionSpec as P

L = 1024
LAG_FIRST = 64
LAG_HALF = 448
LAGS = 2 * LAG_HALF
NZ, NH, NK = 8, 2, 2
NX, NY = 2, 4
NF = NX * NY
FINAL_BINS = 8
CH = 4
MESH = pl.DeviceIdType.MESH
BF16 = jnp.bfloat16
F32 = jnp.float32


def lag_constants(freq_total, freq_dev):
    reach = LAG_FIRST + np.arange(LAG_HALF, dtype=np.int64)
    lags = np.concatenate([reach, L - reach])
    bins = np.arange(freq_total, dtype=np.int64) + 1
    steps = bins[:, None] * lags[None, :] % L
    angles = steps.astype(np.float32) * np.float32(2.0 * math.pi / L)
    both = np.stack([np.cos(angles), -np.sin(angles)])
    both = both.reshape(2, NF, 2, freq_dev // 2, LAGS).transpose(1, 2, 0, 3, 4)
    both = both.reshape(2 * freq_total, LAGS)
    inverse = (both.T * np.float32(1.0 / math.sqrt(freq_total))).astype(ml_dtypes.bfloat16)
    forward = (both * np.float32(4.0 / math.sqrt(L))).astype(ml_dtypes.bfloat16)
    swap = np.zeros((256, 256), np.float32)
    for a in range(16):
        for b in range(16):
            swap[a * 16 + b, b * 16 + a] = 1.0
    piece = np.zeros((128, 512), np.float32)
    for v in range(4):
        for f in range(16):
            for part in range(2):
                piece[(v * 16 + f) * 2 + part, part * 256 + f * 16 + v] = 1.0
    return inverse, forward, swap.astype(ml_dtypes.bfloat16), piece.astype(ml_dtypes.bfloat16)


def dot(a, b):
    return jnp.dot(a, b, preferred_element_type=F32)


def dot_nt(a, b):
    return lax.dot_general(a, b, (((1,), (1,)), ((), ())), preferred_element_type=F32)


def onehot_rows(idx_ref, first, count, base):
    row = lax.broadcasted_iota(jnp.int32, (16, 256), 0)
    lane = lax.broadcasted_iota(jnp.int32, (16, 256), 1)
    out = jnp.zeros((16, 256), F32)
    for i in range(count):
        hit = (row == i) & (lane == idx_ref[first + i] - base)
        out = jnp.where(hit, 1.0, out)
    return out.astype(BF16)


def c3_kernel(
    vs_ref, rf_ref, cs_ref, ce_ref, inv_hbm, fwd_hbm, swap_hbm, piece_hbm, spec_hbm,
    rel_hbm, pick_hbm,
    spec, bank, ag_a, left, mix, send1, recv1, send2, recv2, series, squashed, tap, rel, ag_b,
    inv_ref, fwd_ref, swap_ref, piece_ref, load_sem, out_sem,
    a1s, a1r, a2s, a2r, a3s, a3r,
    d0s, d0r, d1s, d1r, d2s, d2r,
    x1s, x1r, x2s, x2r,
):
    mr = lax.axis_index("rcv")
    mf = lax.axis_index("frq")
    mz, mh, mk = mr // 4, (mr // 2) % 2, mr % 2
    mx, my = mf // NY, mf % NY

    def rcv_of(z, h, k):
        return (z * NH + h) * NK + k

    plane_peers = [
        (rcv_of((mz + o) % NZ, (mh + p) % NH, mk), mf)
        for p in range(NH)
        for o in (4, 3, 5, 2, 6, 1, 7, 0)
        if o or p
    ]
    h_peer = (rcv_of(mz, 1 - mh, mk), mf)
    k_peer = (rcv_of(mz, mh, 1 - mk), mf)
    f_shift = [(dx, dy) for dx in range(NX) for dy in range(NY) if dx or dy]
    f_peers = [((mx + dx) % NX) * NY + (my + dy) % NY for dx, dy in f_shift]

    barrier = pltpu.get_barrier_semaphore()
    peers = plane_peers + [k_peer] + [(mr, j) for j in f_peers]
    for peer in peers:
        pl.semaphore_signal(barrier, inc=1, device_id=peer, device_id_type=MESH)

    loads = [
        pltpu.make_async_copy(
            spec_hbm.at[pl.ds(i * 64, 64)], spec.at[pl.ds(i * 64, 64)], load_sem.at[i]
        )
        for i in range(8)
    ]
    tables = [
        pltpu.make_async_copy(inv_hbm, inv_ref, load_sem.at[8]),
        pltpu.make_async_copy(fwd_hbm, fwd_ref, load_sem.at[9]),
    ]
    early = [
        pltpu.make_async_copy(swap_hbm, swap_ref, load_sem.at[10]),
        pltpu.make_async_copy(piece_hbm, piece_ref, load_sem.at[11]),
    ]
    for load in early + loads + tables:
        load.start()
    for load in early:
        load.wait()

    def swapped(block):
        return dot(swap_ref[...], block)

    for i in range(8):
        loads[i].wait()

        def relay(n, _):
            off = pl.multiple_of(n * 16, 16)
            block = spec[pl.ds(off, 16)].reshape(256, 256)
            bank[:, pl.ds(off, 16), :] = swapped(block).astype(BF16).reshape(16, 16, 256)
            return 0

        lax.fori_loop(i * 4, i * 4 + 4, relay, 0, unroll=4)

    pick_v = onehot_rows(vs_ref, mr * 4, 4, mr * 256)

    def select(f, _):
        mix_rows = dot_nt(pick_v, bank[f]).astype(BF16)
        left[f, 0:16, :] = mix_rows
        return 0

    lax.fori_loop(0, 16, select, 0, unroll=4)
    chosen = jnp.concatenate(
        [left[:, 0:16, 0:256].reshape(256, 256), left[:, 0:16, 256:512].reshape(256, 256)], axis=0
    )
    chosen = dot(piece_ref[...], chosen).astype(BF16)
    for c in range(CH):
        for half in range(2):
            at = c * 32 + half * 16
            ag_a[c, half, mz, mh, mk] = chosen[at : at + 16]

    def remote(src, dst, ssem, rsem, dev):
        return pltpu.make_async_remote_copy(
            src_ref=src, dst_ref=dst, send_sem=ssem, recv_sem=rsem,
            device_id=dev, device_id_type=MESH,
        )

    def z_peer(o):
        return rcv_of((mz + o) % NZ, mh, mk), mf

    class Group:
        def __init__(self, copies, whole, ssem, rsem):
            self.copies = copies
            self.whole = whole
            self.ssem = ssem
            self.rsem = rsem

        def start(self):
            for copy in self.copies:
                copy.start()

        def wait_send(self):
            pltpu.make_async_copy(self.whole, self.whole, self.ssem).wait()

        def wait_recv(self):
            pltpu.make_async_copy(self.whole, self.whole, self.rsem).wait()

    class Gather:
        def __init__(self, view, sems, out_view=None, out_sem=None):
            s1, r1, s2, r2, s3, r3 = sems
            one = view(mz, mh, mk)
            self.first = remote(one, one, s1, r1, h_peer)
            two = view(mz, slice(None), mk)
            self.near = [
                remote(two, two, s2, r2.at[min(i, 2)], z_peer(o))
                for i, o in enumerate((2, -2, 1, -1))
            ]
            self.far = []
            for i, o in enumerate((1, -1)):
                two = view((mz - 2 * o) % NZ, slice(None), mk)
                one = view((mz - 2 * o) % NZ, i, mk)
                self.far.append(
                    [
                        remote(two, two, s2, r2.at[2], z_peer(o)),
                        remote(one, one, s2, r2.at[2], z_peer(2 * o)),
                    ]
                )
            self.all_sent = Group([], view(pl.ds(0, 7), slice(None), mk), s2, s2)
            self.rest = Group([], view(pl.ds(0, 5), slice(None), mk), s2, r2.at[2])
            half = view(slice(None), slice(None), mk)
            landing = half if out_view is None else out_view(slice(None), slice(None), mk)
            self.third = remote(half, landing, s3, r3, k_peer)
            self.local = None
            if out_view is not None:
                self.local = pltpu.make_async_copy(half, landing, out_sem)

        def start1(self):
            self.first.wait_recv()
            for copy in self.near:
                copy.start()

        def start2(self):
            for i in range(2):
                self.near[i].wait_recv()
                for copy in self.far[i]:
                    copy.start()

        def start3(self):
            self.rest.wait_recv()
            self.third.start()
            if self.local is not None:
                self.local.start()

        def finish(self):
            self.first.wait_send()
            self.all_sent.wait_send()
            self.third.wait_send()
            if self.local is not None:
                self.third.wait_recv()
                self.local.wait()

    class Direct:
        def __init__(self, view, sems, out_view=None, out_sem=None, plane=False):
            s0, r0, s1, r1, s3, r3 = sems
            one = view(mz, mh, mk)
            if plane:
                self.first = None
                copies = [remote(one, one, s1, r1, peer) for peer in plane_peers]
                whole = send1.at[0, pl.ds(0, len(copies)), pl.ds(0, 16), :]
            else:
                self.first = remote(one, one, s0, r0, h_peer)
                two = view(mz, slice(None), mk)
                copies = [remote(two, two, s1, r1, z_peer(o)) for o in (4, 3, 5, 2, 6, 1, 7)]
                whole = view(pl.ds(0, NZ - 1), slice(None), mk)
            self.near = Group(copies, whole, s1, r1)
            half = view(slice(None), slice(None), mk)
            landing = half if out_view is None else out_view(slice(None), slice(None), mk)
            self.third = remote(half, landing, s3, r3, k_peer)
            self.local = None
            if out_view is not None:
                self.local = pltpu.make_async_copy(half, landing, out_sem)

        def start1(self):
            if self.first is not None:
                self.first.wait_recv()
            self.near.start()

        def start3(self):
            self.near.wait_recv()
            self.third.start()
            if self.local is not None:
                self.local.start()

        def finish(self):
            if self.first is not None:
                self.first.wait_send()
            self.near.wait_send()
            self.third.wait_send()
            if self.local is not None:
                self.third.wait_recv()
                self.local.wait()

    def pair_sems(c, s1, r1, s2, r2, s3, r3):
        return s1.at[c], r1.at[c], s2.at[c], r2.at[c], s3.at[c], r3.at[c]

    def direct_sems(n):
        return d0s.at[n], d0r.at[n], d1s.at[n], d1r.at[n], d2s.at[n], d2r.at[n]

    da = [
        Direct(
            lambda z, h, k, half=half: ag_a.at[0, half, z, h, k],
            direct_sems(half),
            plane=True,
        )
        for half in range(2)
    ]
    ga = [None] + [
        Gather(
            lambda z, h, k, c=c: ag_a.at[c, :, z, h, k],
            pair_sems(c - 1, a1s, a1r, a2s, a2r, a3s, a3r),
        )
        for c in range(1, CH)
    ]
    def pick_gather(n, first, count):
        view = lambda z, h, k: ag_b.at[z, h, k, :, pl.ds(first, count)]
        out_view = lambda z, h, k: pick_hbm.at[z, h, k, :, pl.ds(first, count)]
        if n == CH - 2:
            sems = pair_sems(CH - 1, a1s, a1r, a2s, a2r, a3s, a3r)
            return Gather(view, sems, out_view, out_sem.at[2, n])
        return Direct(view, direct_sems(2 + n), out_view, out_sem.at[2, n], plane=n == CH)

    db = [pick_gather(c, c * 1024, 1024) for c in range(CH - 1)]
    db = db + [pick_gather(CH - 1 + half, 3072 + half * 512, 512) for half in range(2)]

    pl.semaphore_wait(barrier, len(peers))
    da[0].start1()
    for gather in ga[1:]:
        gather.first.start()

    reach = LAG_FIRST + lax.broadcasted_iota(jnp.int32, (LAG_HALF, 128), 0)
    first, last = cs_ref[...], ce_ref[...]
    inside = (reach >= first) & (reach < last)
    span = (last - first).astype(F32)
    sine = jnp.sin(math.pi * ((reach - first).astype(F32) + 0.5) / span)
    weights = jnp.where(inside, sine * sine, 0.0)
    weights = pltpu.roll(weights, (128 - 16 * mf) % 128, 1)
    for v in range(16):
        tap[v] = jnp.broadcast_to(weights[:, v : v + 1], (LAG_HALF, 128))
    da[1].start1()

    def rows(j):
        return pl.ds(pl.multiple_of(j * 32, 32), 32)

    def part_rows(j, half):
        return pl.ds(pl.multiple_of(j * 32 + half * 16, 16), 16)

    def quad(j):
        return pl.ds(pl.multiple_of(j * 4, 4), 4)

    def exchange(n, src, dst, whole, ssem, rsem):
        copies = [remote(src(j), dst(mf), ssem.at[n], rsem.at[n], (mr, j)) for j in f_peers]
        return [Group(copies, whole, ssem.at[n], rsem.at[n])]

    whole_half = send1.at[0, pl.ds(0, 4 * (NF - 1)), pl.ds(0, 16), :]

    ex1 = [
        [
            exchange(
                2 * c + half,
                lambda j, c=c, half=half: send1.at[c, quad(j), pl.ds(half * 16, 16), :],
                lambda j, c=c, half=half: recv1.at[c, :, part_rows(j, half), :],
                whole_half, x1s, x1r,
            )
            for half in range(2)
        ]
        for c in range(CH)
    ]
    ex2 = [
        [
            exchange(
                2 * c + half,
                lambda j, c=c, half=half: send2.at[c, :, part_rows(j, half), :],
                lambda j, c=c, half=half: recv2.at[c, quad(j), pl.ds(half * 16, 16), :],
                whole_half, x2s, x2r,
            )
            for half in range(2)
        ]
        for c in range(CH)
    ]

    def send(group):
        for copy in group:
            copy.start()

    def sent(group):
        for copy in group:
            copy.wait_send()

    def give_back(c, half):
        send(ex2[c][half])

    def cross_half(c, half):
        first = half * 8
        for g in range(2):
            block = swapped(ag_a[c, half, g * 4 : g * 4 + 4].reshape(256, 256))
            plain = block.astype(BF16).reshape(8, 2, 16, 256)
            minus = (-block).astype(BF16).reshape(8, 2, 16, 256)
            at = g * 16
            left[first : first + 8, at : at + 16, 0:256] = plain[:, 0]
            left[first : first + 8, at : at + 16, 256:512] = plain[:, 1]
            left[first : first + 8, 32 + at : 48 + at, 0:256] = minus[:, 1]
            left[first : first + 8, 32 + at : 48 + at, 256:512] = plain[:, 0]

        def one_bin(f, _):
            out = (dot(left[first + f], bank[first + f]) * 0.0625).astype(BF16)
            out = out.reshape(4, 16, 256)
            for part in range(2):
                off = pl.multiple_of(part * 128 + f * 16, 16)
                mix[half, :, pl.ds(off, 16), :] = out[part * 2 : part * 2 + 2]
            return 0

        lax.fori_loop(0, 8, one_bin, 0, unroll=4)
        for g in range(2):
            block = swapped(mix[half, g]).astype(BF16)
            send1[c, g * 16 : g * 16 + 16, half * 16 : half * 16 + 16, :] = block.reshape(
                16, 16, 256
            )

    def cross_first(half):
        da[half].third.wait_recv()
        cross_half(0, half)
        send(ex1[0][half])
        recv1[0, :, part_rows(mf, half), :] = send1[0, quad(mf), half * 16 : half * 16 + 16, :]

    def cross(c):
        ga[c].third.wait_recv()
        for half in range(2):
            cross_half(c, half)
            send(ex1[c][half])
        recv1[c, :, rows(mf), :] = send1[c, quad(mf)]

    def lag_step(c):
        for copy in ex1[c][0] + ex1[c][1]:
            copy.wait_recv()

        def two_sources(pair, _):
            for i in range(2):
                q = pair * 2 + i
                series[i] = dot(inv_ref[...], recv1[c, q])
                for n in range(7):
                    w = tap[q * 4 + c, n * 64 : n * 64 + 64, :]
                    w = jnp.concatenate([w, w], axis=1)
                    for h in range(2):
                        at = h * LAG_HALF + n * 64
                        x = series[i, at : at + 64, :] * w
                        squashed[i, at : at + 64, :] = (x * lax.rsqrt(1.0 + x * x)).astype(BF16)
                send2[c, q] = dot(fwd_ref[...], squashed[i]).astype(BF16)
            return 0

        lax.fori_loop(0, 2, two_sources, 0)
        recv2[c, quad(mf)] = send2[c, :, rows(mf), :]

    pick_p = onehot_rows(rf_ref, mr * 8, 8, mr * 256)
    outs = []

    def turn_half(c, half):
        first = half * 8
        for g in range(2):
            block = recv2[c, g * 16 : g * 16 + 16, half * 16 : half * 16 + 16, :]
            block = swapped(block.reshape(256, 256)).astype(BF16).reshape(2, 8, 16, 256)
            for part in range(2):
                at = c * 64 + part * 32 + g * 16
                rel[first : first + 8, at : at + 16, :] = block[part]
        out = pltpu.make_async_copy(
            rel.at[pl.ds(first, 8), pl.ds(c * 64, 64), :],
            rel_hbm.at[pl.ds(first, 8), pl.ds(c * 64, 64), :],
            out_sem.at[half, c],
        )
        out.start()
        outs.append(out)
        for n in range(half * 2, half * 2 + 2):
            order = (1, 0, 3, 2) if c % 2 else (0, 1, 2, 3)
            block = [rel[n * 4 + i, c * 64 : c * 64 + 64, :] for i in order]
            block = jnp.concatenate(block, axis=0)
            got = dot_nt(pick_p, block)[0:8].astype(BF16)
            ag_b[mz, mh, mk, :, c * 1024 + n * 256 : c * 1024 + n * 256 + 256] = got

    def turn_step(c):
        for copy in ex2[c][0] + ex2[c][1]:
            copy.wait_recv()
        turn_half(c, 0)
        turn_half(c, 1)
        db[c].first.start()

    def turn_last(half):
        for copy in ex2[CH - 1][half]:
            copy.wait_recv()
        turn_half(CH - 1, half)
        if half == 0:
            db[CH - 1].first.start()
        else:
            db[CH].start1()

    da[0].start3()
    ga[1].start1()
    cross_first(0)
    da[1].start3()
    ga[1].start2()
    ga[2].start1()
    cross_first(1)
    ga[1].start3()
    ga[2].start2()
    ga[3].start1()
    cross(1)
    ga[2].start3()
    ga[3].start2()
    cross(2)
    ga[3].start3()
    for table in tables:
        table.wait()
    lag_step(0)
    give_back(0, 0)
    give_back(0, 1)
    cross(3)
    lag_step(1)
    give_back(1, 0)
    for gather in da + ga[1:]:
        gather.finish()
    for c in range(CH - 1):
        sent(ex1[c][0] + ex1[c][1])
    turn_step(0)
    give_back(1, 1)
    lag_step(2)
    give_back(2, 0)
    sent(ex1[3][0] + ex1[3][1] + ex2[0][0] + ex2[0][1])
    db[0].start1()
    turn_step(1)
    give_back(2, 1)
    lag_step(3)
    give_back(3, 0)
    db[1].start1()
    db[0].start3()
    turn_step(2)
    give_back(3, 1)
    sent(ex2[1][0] + ex2[1][1])
    db[0].finish()
    db[2].start1()
    turn_last(0)
    db[1].start3()
    turn_last(1)
    db[3].start1()
    db[2].start2()
    sent(ex2[2][0] + ex2[2][1])
    db[1].finish()
    db[2].start3()
    db[3].start3()
    db[4].start3()

    for c in range(2, CH + 1):
        db[c].finish()
    sent(ex2[3][0] + ex2[3][1])
    for out in outs:
        out.wait()


def final_kernel(scale, p0, p1, p2, p3, rel_ref, out_ref):
    low = lax.broadcasted_iota(jnp.int32, (256, 128), 1) < 64
    for b in range(FINAL_BINS):
        odd = b % 2
        lanes = slice(b // 2 * 128, b // 2 * 128 + 128)
        pieces = [p[:, lanes] for p in (p0, p1, p2, p3)]
        left, real, imag = [], [], []
        for c in range(CH):
            if c % 2 == 0:
                left.append(jnp.where(low, pieces[c + odd], pieces[c + 1 - odd]))
            at = (c ^ odd) * 64
            one, other = rel_ref[b, at : at + 32, :], rel_ref[b, at + 32 : at + 64, :]
            real += [one, other]
            imag += [other, -one]
        left = jnp.concatenate(left, axis=1)
        out_ref[0, b] = dot(left, jnp.concatenate(real, axis=0)) * scale
        out_ref[1, b] = dot(left, jnp.concatenate(imag, axis=0)) * scale


def per_device(spectra, virtual_sources, references, coda_start, coda_end):
    windows, freq_dev, rcv_dev = spectra.shape[1:]
    sources = virtual_sources.shape[0]
    picks = references.shape[0]
    inverse, forward, swap, piece = lag_constants(freq_dev * NF, freq_dev)
    vmem = pl.BlockSpec(memory_space=pltpu.VMEM)
    smem = pl.BlockSpec(memory_space=pltpu.SMEM)
    hbm = pl.BlockSpec(memory_space=pl.ANY)
    dma = pltpu.SemaphoreType.DMA
    gather_sems = [dma((CH,))] * 3 + [dma((CH, 3))] + [dma((CH,))] * 2
    rel, picked = pl.pallas_call(
        c3_kernel,
        out_shape=(
            jax.ShapeDtypeStruct((16, 256, 256), BF16),
            jax.ShapeDtypeStruct((NZ, NH, NK, 8, 4096), BF16),
        ),
        in_specs=[smem, smem, vmem, vmem, hbm, hbm, hbm, hbm, hbm],
        out_specs=(hbm, hbm),
        scratch_shapes=[
            pltpu.VMEM((512, 16, 256), BF16),
            pltpu.VMEM((16, 512, 256), BF16),
            pltpu.VMEM((CH, 2, NZ, NH, NK, 16, 256), BF16),
            pltpu.VMEM((16, 64, 512), BF16),
            pltpu.VMEM((2, 2, 256, 256), BF16),
            pltpu.VMEM((CH, 32, 32, 256), BF16),
            pltpu.VMEM((CH, 4, 256, 256), BF16),
            pltpu.VMEM((CH, 4, 256, 256), BF16),
            pltpu.VMEM((CH, 32, 32, 256), BF16),
            pltpu.VMEM((2, LAGS, 256), F32),
            pltpu.VMEM((2, LAGS, 256), BF16),
            pltpu.VMEM((16, LAG_HALF, 128), F32),
            pltpu.VMEM((16, 256, 256), BF16),
            pltpu.VMEM((NZ, NH, NK, 8, 4096), BF16),
            pltpu.VMEM((LAGS, 256), BF16),
            pltpu.VMEM((256, LAGS), BF16),
            pltpu.VMEM((256, 256), BF16),
            pltpu.VMEM((128, 512), BF16),
            dma((12,)),
            dma((3, CH + 1)),
        ]
        + gather_sems
        + [dma((CH + 3,))] * 2
        + [dma((CH + 3,))] * 2
        + [dma((CH + 3,))] * 2
        + [dma((2 * CH,))] * 4,
        compiler_params=pltpu.CompilerParams(
            collective_id=0, has_side_effects=True, vmem_limit_bytes=56 << 20
        ),
        name="c3_exchange",
    )(
        virtual_sources,
        references,
        coda_start.reshape(1, sources),
        coda_end.reshape(1, sources),
        jnp.asarray(inverse),
        jnp.asarray(forward),
        jnp.asarray(swap),
        jnp.asarray(piece),
        spectra.reshape(2 * windows, freq_dev, rcv_dev),
    )
    picked = picked.reshape(picks, 4096)
    steps = freq_dev // FINAL_BINS
    lane_block = lambda c: pl.BlockSpec(
        (256, 64 * FINAL_BINS), lambda n: (0, c * steps + n)
    )
    return pl.pallas_call(
        functools.partial(final_kernel, 1.0 / math.sqrt(sources)),
        grid=(steps,),
        out_shape=jax.ShapeDtypeStruct((2, freq_dev, picks, rcv_dev), F32),
        in_specs=[lane_block(c) for c in range(CH)]
        + [pl.BlockSpec((FINAL_BINS, 256, 256), lambda n: (n, 0, 0))],
        out_specs=pl.BlockSpec((2, FINAL_BINS, 256, 256), lambda n: (0, n, 0, 0)),
        compiler_params=pltpu.CompilerParams(vmem_limit_bytes=60 << 20),
        name="recorrelate",
    )(picked, picked, picked, picked, rel)


def solution(mesh):
    return jax.shard_map(
        per_device,
        mesh=mesh,
        in_specs=(P(None, None, "frq", "rcv"), P(), P(), P(), P()),
        out_specs=P(None, "frq", None, "rcv"),
        check_vma=False,
    )
```

```python
import functools
import math

import jax
import jax.numpy as jnp
import ml_dtypes
import numpy as np
from jax import lax
from jax.experimental import pallas as pl
from jax.experimental.pallas import tpu as pltpu
from jax.sharding import PartitionSpec as P

L = 1024
LAG_FIRST = 64
LAG_HALF = 448
LAGS = 2 * LAG_HALF
NZ, NH, NK = 8, 2, 2
NX, NY = 2, 4
NF = NX * NY
FINAL_BINS = 8
CH = 4
MESH = pl.DeviceIdType.MESH
BF16 = jnp.bfloat16
F32 = jnp.float32


def lag_constants(freq_total, freq_dev):
    reach = LAG_FIRST + np.arange(LAG_HALF, dtype=np.int64)
    lags = np.concatenate([reach, L - reach])
    bins = np.arange(freq_total, dtype=np.int64) + 1
    steps = bins[:, None] * lags[None, :] % L
    angles = steps.astype(np.float32) * np.float32(2.0 * math.pi / L)
    both = np.stack([np.cos(angles), -np.sin(angles)])
    both = both.reshape(2, NF, 2, freq_dev // 2, LAGS).transpose(1, 2, 0, 3, 4)
    both = both.reshape(2 * freq_total, LAGS)
    inverse = (both.T * np.float32(1.0 / math.sqrt(freq_total))).astype(ml_dtypes.bfloat16)
    forward = (both * np.float32(4.0 / math.sqrt(L))).astype(ml_dtypes.bfloat16)
    swap = np.zeros((256, 256), np.float32)
    for a in range(16):
        for b in range(16):
            swap[a * 16 + b, b * 16 + a] = 1.0
    piece = np.zeros((128, 512), np.float32)
    for v in range(4):
        for f in range(16):
            for part in range(2):
                piece[(v * 16 + f) * 2 + part, part * 256 + f * 16 + v] = 1.0
    return inverse, forward, swap.astype(ml_dtypes.bfloat16), piece.astype(ml_dtypes.bfloat16)


def dot(a, b):
    return jnp.dot(a, b, preferred_element_type=F32)


def dot_nt(a, b):
    return lax.dot_general(a, b, (((1,), (1,)), ((), ())), preferred_element_type=F32)


def onehot_rows(idx_ref, first, count, base):
    row = lax.broadcasted_iota(jnp.int32, (16, 256), 0)
    lane = lax.broadcasted_iota(jnp.int32, (16, 256), 1)
    out = jnp.zeros((16, 256), F32)
    for i in range(count):
        hit = (row == i) & (lane == idx_ref[first + i] - base)
        out = jnp.where(hit, 1.0, out)
    return out.astype(BF16)


def c3_kernel(
    vs_ref, rf_ref, cs_ref, ce_ref, inv_hbm, fwd_hbm, swap_hbm, piece_hbm, spec_hbm,
    rel_hbm, pick_hbm,
    spec, bank, ag_a, left, mix, send1, recv1, send2, recv2, series, squashed, tap, rel, ag_b,
    inv_ref, fwd_ref, swap_ref, piece_ref, load_sem, out_sem,
    a1s, a1r, a2s, a2r, a3s, a3r,
    d0s, d0r, d1s, d1r, d2s, d2r,
    x1s, x1r, x2s, x2r,
):
    mr = lax.axis_index("rcv")
    mf = lax.axis_index("frq")
    mz, mh, mk = mr // 4, (mr // 2) % 2, mr % 2
    mx, my = mf // NY, mf % NY

    def rcv_of(z, h, k):
        return (z * NH + h) * NK + k

    plane_peers = [
        (rcv_of((mz + o) % NZ, (mh + p) % NH, mk), mf)
        for p in range(NH)
        for o in (4, 3, 5, 2, 6, 1, 7, 0)
        if o or p
    ]
    h_peer = (rcv_of(mz, 1 - mh, mk), mf)
    k_peer = (rcv_of(mz, mh, 1 - mk), mf)
    f_shift = [(dx, dy) for dx in range(NX) for dy in range(NY) if dx or dy]
    f_peers = [((mx + dx) % NX) * NY + (my + dy) % NY for dx, dy in f_shift]

    barrier = pltpu.get_barrier_semaphore()
    peers = plane_peers + [k_peer] + [(mr, j) for j in f_peers]
    for peer in peers:
        pl.semaphore_signal(barrier, inc=1, device_id=peer, device_id_type=MESH)

    loads = [
        pltpu.make_async_copy(
            spec_hbm.at[pl.ds(i * 64, 64)], spec.at[pl.ds(i * 64, 64)], load_sem.at[i]
        )
        for i in range(8)
    ]
    tables = [
        pltpu.make_async_copy(inv_hbm, inv_ref, load_sem.at[8]),
        pltpu.make_async_copy(fwd_hbm, fwd_ref, load_sem.at[9]),
    ]
    early = [
        pltpu.make_async_copy(swap_hbm, swap_ref, load_sem.at[10]),
        pltpu.make_async_copy(piece_hbm, piece_ref, load_sem.at[11]),
    ]
    for load in early + loads + tables:
        load.start()
    for load in early:
        load.wait()

    def swapped(block):
        return dot(swap_ref[...], block)

    for i in range(8):
        loads[i].wait()

        def relay(n, _):
            off = pl.multiple_of(n * 16, 16)
            block = spec[pl.ds(off, 16)].reshape(256, 256)
            bank[:, pl.ds(off, 16), :] = swapped(block).astype(BF16).reshape(16, 16, 256)
            return 0

        lax.fori_loop(i * 4, i * 4 + 4, relay, 0, unroll=4)

    pick_v = onehot_rows(vs_ref, mr * 4, 4, mr * 256)

    def select(f, _):
        mix_rows = dot_nt(pick_v, bank[f]).astype(BF16)
        left[f, 0:16, :] = mix_rows
        return 0

    lax.fori_loop(0, 16, select, 0, unroll=4)
    chosen = jnp.concatenate(
        [left[:, 0:16, 0:256].reshape(256, 256), left[:, 0:16, 256:512].reshape(256, 256)], axis=0
    )
    chosen = dot(piece_ref[...], chosen).astype(BF16)
    for c in range(CH):
        for half in range(2):
            at = c * 32 + half * 16
            ag_a[c, half, mz, mh, mk] = chosen[at : at + 16]

    def remote(src, dst, ssem, rsem, dev):
        return pltpu.make_async_remote_copy(
            src_ref=src, dst_ref=dst, send_sem=ssem, recv_sem=rsem,
            device_id=dev, device_id_type=MESH,
        )

    def z_peer(o):
        return rcv_of((mz + o) % NZ, mh, mk), mf

    class Group:
        def __init__(self, copies, whole, ssem, rsem):
            self.copies = copies
            self.whole = whole
            self.ssem = ssem
            self.rsem = rsem

        def start(self):
            for copy in self.copies:
                copy.start()

        def wait_send(self):
            pltpu.make_async_copy(self.whole, self.whole, self.ssem).wait()

        def wait_recv(self):
            pltpu.make_async_copy(self.whole, self.whole, self.rsem).wait()

    class Gather:
        def __init__(self, view, sems, out_view=None, out_sem=None):
            s1, r1, s2, r2, s3, r3 = sems
            one = view(mz, mh, mk)
            self.first = remote(one, one, s1, r1, h_peer)
            two = view(mz, slice(None), mk)
            self.near = [
                remote(two, two, s2, r2.at[min(i, 2)], z_peer(o))
                for i, o in enumerate((2, -2, 1, -1))
            ]
            self.far = []
            for i, o in enumerate((1, -1)):
                two = view((mz - 2 * o) % NZ, slice(None), mk)
                one = view((mz - 2 * o) % NZ, i, mk)
                self.far.append(
                    [
                        remote(two, two, s2, r2.at[2], z_peer(o)),
                        remote(one, one, s2, r2.at[2], z_peer(2 * o)),
                    ]
                )
            self.all_sent = Group([], view(pl.ds(0, 7), slice(None), mk), s2, s2)
            self.rest = Group([], view(pl.ds(0, 5), slice(None), mk), s2, r2.at[2])
            half = view(slice(None), slice(None), mk)
            landing = half if out_view is None else out_view(slice(None), slice(None), mk)
            self.third = remote(half, landing, s3, r3, k_peer)
            self.local = None
            if out_view is not None:
                self.local = pltpu.make_async_copy(half, landing, out_sem)

        def start1(self):
            self.first.wait_recv()
            for copy in self.near:
                copy.start()

        def start2(self):
            for i in range(2):
                self.near[i].wait_recv()
                for copy in self.far[i]:
                    copy.start()

        def start3(self):
            self.rest.wait_recv()
            self.third.start()
            if self.local is not None:
                self.local.start()

        def finish(self):
            self.first.wait_send()
            self.all_sent.wait_send()
            self.third.wait_send()
            if self.local is not None:
                self.third.wait_recv()
                self.local.wait()

    class Direct:
        def __init__(self, view, sems, out_view=None, out_sem=None, plane=False):
            s0, r0, s1, r1, s3, r3 = sems
            one = view(mz, mh, mk)
            if plane:
                self.first = None
                copies = [remote(one, one, s1, r1, peer) for peer in plane_peers]
                whole = send1.at[0, pl.ds(0, len(copies)), pl.ds(0, 16), :]
            else:
                self.first = remote(one, one, s0, r0, h_peer)
                two = view(mz, slice(None), mk)
                copies = [remote(two, two, s1, r1, z_peer(o)) for o in (4, 3, 5, 2, 6, 1, 7)]
                whole = view(pl.ds(0, NZ - 1), slice(None), mk)
            self.near = Group(copies, whole, s1, r1)
            half = view(slice(None), slice(None), mk)
            landing = half if out_view is None else out_view(slice(None), slice(None), mk)
            self.third = remote(half, landing, s3, r3, k_peer)
            self.local = None
            if out_view is not None:
                self.local = pltpu.make_async_copy(half, landing, out_sem)

        def start1(self):
            if self.first is not None:
                self.first.wait_recv()
            self.near.start()

        def start3(self):
            self.near.wait_recv()
            self.third.start()
            if self.local is not None:
                self.local.start()

        def finish(self):
            if self.first is not None:
                self.first.wait_send()
            self.near.wait_send()
            self.third.wait_send()
            if self.local is not None:
                self.third.wait_recv()
                self.local.wait()

    def pair_sems(c, s1, r1, s2, r2, s3, r3):
        return s1.at[c], r1.at[c], s2.at[c], r2.at[c], s3.at[c], r3.at[c]

    def direct_sems(n):
        return d0s.at[n], d0r.at[n], d1s.at[n], d1r.at[n], d2s.at[n], d2r.at[n]

    da = [
        Direct(
            lambda z, h, k, half=half: ag_a.at[0, half, z, h, k],
            direct_sems(half),
            plane=True,
        )
        for half in range(2)
    ]
    ga = [None] + [
        Gather(
            lambda z, h, k, c=c: ag_a.at[c, :, z, h, k],
            pair_sems(c - 1, a1s, a1r, a2s, a2r, a3s, a3r),
        )
        for c in range(1, CH)
    ]
    def pick_gather(n, first, count):
        view = lambda z, h, k: ag_b.at[z, h, k, :, pl.ds(first, count)]
        out_view = lambda z, h, k: pick_hbm.at[z, h, k, :, pl.ds(first, count)]
        if n == CH - 2:
            sems = pair_sems(CH - 1, a1s, a1r, a2s, a2r, a3s, a3r)
            return Gather(view, sems, out_view, out_sem.at[2, n])
        return Direct(view, direct_sems(2 + n), out_view, out_sem.at[2, n], plane=n >= CH - 1)

    db = [pick_gather(c, c * 1024, 1024) for c in range(CH - 1)]
    db = db + [pick_gather(CH - 1 + half, 3072 + half * 512, 512) for half in range(2)]

    pl.semaphore_wait(barrier, len(peers))
    da[0].start1()
    for gather in ga[1:]:
        gather.first.start()

    reach = LAG_FIRST + lax.broadcasted_iota(jnp.int32, (LAG_HALF, 128), 0)
    first, last = cs_ref[...], ce_ref[...]
    inside = (reach >= first) & (reach < last)
    span = (last - first).astype(F32)
    sine = jnp.sin(math.pi * ((reach - first).astype(F32) + 0.5) / span)
    weights = jnp.where(inside, sine * sine, 0.0)
    weights = pltpu.roll(weights, (128 - 16 * mf) % 128, 1)
    for v in range(16):
        tap[v] = jnp.broadcast_to(weights[:, v : v + 1], (LAG_HALF, 128))
    da[1].start1()

    def rows(j):
        return pl.ds(pl.multiple_of(j * 32, 32), 32)

    def part_rows(j, half):
        return pl.ds(pl.multiple_of(j * 32 + half * 16, 16), 16)

    def quad(j):
        return pl.ds(pl.multiple_of(j * 4, 4), 4)

    def exchange(n, src, dst, whole, ssem, rsem):
        copies = [remote(src(j), dst(mf), ssem.at[n], rsem.at[n], (mr, j)) for j in f_peers]
        return [Group(copies, whole, ssem.at[n], rsem.at[n])]

    whole_half = send1.at[0, pl.ds(0, 4 * (NF - 1)), pl.ds(0, 16), :]

    ex1 = [
        [
            exchange(
                2 * c + half,
                lambda j, c=c, half=half: send1.at[c, quad(j), pl.ds(half * 16, 16), :],
                lambda j, c=c, half=half: recv1.at[c, :, part_rows(j, half), :],
                whole_half, x1s, x1r,
            )
            for half in range(2)
        ]
        for c in range(CH)
    ]
    ex2 = [
        [
            exchange(
                2 * c + half,
                lambda j, c=c, half=half: send2.at[c, :, part_rows(j, half), :],
                lambda j, c=c, half=half: recv2.at[c, quad(j), pl.ds(half * 16, 16), :],
                whole_half, x2s, x2r,
            )
            for half in range(2)
        ]
        for c in range(CH)
    ]

    def send(group):
        for copy in group:
            copy.start()

    def sent(group):
        for copy in group:
            copy.wait_send()

    def give_back(c, half):
        send(ex2[c][half])

    def cross_half(c, half):
        first = half * 8
        for g in range(2):
            block = swapped(ag_a[c, half, g * 4 : g * 4 + 4].reshape(256, 256))
            plain = block.astype(BF16).reshape(8, 2, 16, 256)
            minus = (-block).astype(BF16).reshape(8, 2, 16, 256)
            at = g * 16
            left[first : first + 8, at : at + 16, 0:256] = plain[:, 0]
            left[first : first + 8, at : at + 16, 256:512] = plain[:, 1]
            left[first : first + 8, 32 + at : 48 + at, 0:256] = minus[:, 1]
            left[first : first + 8, 32 + at : 48 + at, 256:512] = plain[:, 0]

        def one_bin(f, _):
            out = (dot(left[first + f], bank[first + f]) * 0.0625).astype(BF16)
            out = out.reshape(4, 16, 256)
            for part in range(2):
                off = pl.multiple_of(part * 128 + f * 16, 16)
                mix[half, :, pl.ds(off, 16), :] = out[part * 2 : part * 2 + 2]
            return 0

        lax.fori_loop(0, 8, one_bin, 0, unroll=4)
        for g in range(2):
            block = swapped(mix[half, g]).astype(BF16)
            send1[c, g * 16 : g * 16 + 16, half * 16 : half * 16 + 16, :] = block.reshape(
                16, 16, 256
            )

    def cross_first(half):
        da[half].third.wait_recv()
        cross_half(0, half)
        send(ex1[0][half])
        recv1[0, :, part_rows(mf, half), :] = send1[0, quad(mf), half * 16 : half * 16 + 16, :]

    def cross(c):
        ga[c].third.wait_recv()
        for half in range(2):
            cross_half(c, half)
            send(ex1[c][half])
        recv1[c, :, rows(mf), :] = send1[c, quad(mf)]

    def lag_step(c):
        for copy in ex1[c][0] + ex1[c][1]:
            copy.wait_recv()

        def two_sources(pair, _):
            for i in range(2):
                q = pair * 2 + i
                series[i] = dot(inv_ref[...], recv1[c, q])
                for n in range(7):
                    w = tap[q * 4 + c, n * 64 : n * 64 + 64, :]
                    w = jnp.concatenate([w, w], axis=1)
                    for h in range(2):
                        at = h * LAG_HALF + n * 64
                        x = series[i, at : at + 64, :] * w
                        squashed[i, at : at + 64, :] = (x * lax.rsqrt(1.0 + x * x)).astype(BF16)
                send2[c, q] = dot(fwd_ref[...], squashed[i]).astype(BF16)
            return 0

        lax.fori_loop(0, 2, two_sources, 0)
        recv2[c, quad(mf)] = send2[c, :, rows(mf), :]

    pick_p = onehot_rows(rf_ref, mr * 8, 8, mr * 256)
    outs = []

    def turn_half(c, half):
        first = half * 8
        for g in range(2):
            block = recv2[c, g * 16 : g * 16 + 16, half * 16 : half * 16 + 16, :]
            block = swapped(block.reshape(256, 256)).astype(BF16).reshape(2, 8, 16, 256)
            for part in range(2):
                at = c * 64 + part * 32 + g * 16
                rel[first : first + 8, at : at + 16, :] = block[part]
        out = pltpu.make_async_copy(
            rel.at[pl.ds(first, 8), pl.ds(c * 64, 64), :],
            rel_hbm.at[pl.ds(first, 8), pl.ds(c * 64, 64), :],
            out_sem.at[half, c],
        )
        out.start()
        outs.append(out)
        for n in range(half * 2, half * 2 + 2):
            order = (1, 0, 3, 2) if c % 2 else (0, 1, 2, 3)
            block = [rel[n * 4 + i, c * 64 : c * 64 + 64, :] for i in order]
            block = jnp.concatenate(block, axis=0)
            got = dot_nt(pick_p, block)[0:8].astype(BF16)
            ag_b[mz, mh, mk, :, c * 1024 + n * 256 : c * 1024 + n * 256 + 256] = got

    def turn_step(c):
        for copy in ex2[c][0] + ex2[c][1]:
            copy.wait_recv()
        turn_half(c, 0)
        turn_half(c, 1)
        db[c].first.start()

    def turn_last(half):
        for copy in ex2[CH - 1][half]:
            copy.wait_recv()
        turn_half(CH - 1, half)
        db[CH - 1 + half].start1()

    da[0].start3()
    ga[1].start1()
    cross_first(0)
    da[1].start3()
    ga[1].start2()
    ga[2].start1()
    cross_first(1)
    ga[1].start3()
    ga[2].start2()
    ga[3].start1()
    cross(1)
    ga[2].start3()
    ga[3].start2()
    cross(2)
    ga[3].start3()
    for table in tables:
        table.wait()
    lag_step(0)
    give_back(0, 0)
    give_back(0, 1)
    cross(3)
    lag_step(1)
    give_back(1, 0)
    for gather in da + ga[1:]:
        gather.finish()
    for c in range(CH - 1):
        sent(ex1[c][0] + ex1[c][1])
    turn_step(0)
    give_back(1, 1)
    lag_step(2)
    give_back(2, 0)
    sent(ex1[3][0] + ex1[3][1] + ex2[0][0] + ex2[0][1])
    db[0].start1()
    turn_step(1)
    give_back(2, 1)
    lag_step(3)
    give_back(3, 0)
    db[1].start1()
    db[0].start3()
    turn_step(2)
    give_back(3, 1)
    sent(ex2[1][0] + ex2[1][1])
    db[0].finish()
    db[2].start1()
    turn_last(0)
    db[1].start3()
    turn_last(1)
    db[2].start2()
    sent(ex2[2][0] + ex2[2][1])
    db[1].finish()
    db[2].start3()
    db[3].start3()
    db[4].start3()

    for c in range(2, CH + 1):
        db[c].finish()
    sent(ex2[3][0] + ex2[3][1])
    for out in outs:
        out.wait()


def final_kernel(scale, p0, p1, p2, p3, rel_ref, out_ref):
    low = lax.broadcasted_iota(jnp.int32, (256, 128), 1) < 64
    for b in range(FINAL_BINS):
        odd = b % 2
        lanes = slice(b // 2 * 128, b // 2 * 128 + 128)
        pieces = [p[:, lanes] for p in (p0, p1, p2, p3)]
        left, real, imag = [], [], []
        for c in range(CH):
            if c % 2 == 0:
                left.append(jnp.where(low, pieces[c + odd], pieces[c + 1 - odd]))
            at = (c ^ odd) * 64
            one, other = rel_ref[b, at : at + 32, :], rel_ref[b, at + 32 : at + 64, :]
            real += [one, other]
            imag += [other, -one]
        left = jnp.concatenate(left, axis=1)
        out_ref[0, b] = dot(left, jnp.concatenate(real, axis=0)) * scale
        out_ref[1, b] = dot(left, jnp.concatenate(imag, axis=0)) * scale


def per_device(spectra, virtual_sources, references, coda_start, coda_end):
    windows, freq_dev, rcv_dev = spectra.shape[1:]
    sources = virtual_sources.shape[0]
    picks = references.shape[0]
    inverse, forward, swap, piece = lag_constants(freq_dev * NF, freq_dev)
    vmem = pl.BlockSpec(memory_space=pltpu.VMEM)
    smem = pl.BlockSpec(memory_space=pltpu.SMEM)
    hbm = pl.BlockSpec(memory_space=pl.ANY)
    dma = pltpu.SemaphoreType.DMA
    gather_sems = [dma((CH,))] * 3 + [dma((CH, 3))] + [dma((CH,))] * 2
    rel, picked = pl.pallas_call(
        c3_kernel,
        out_shape=(
            jax.ShapeDtypeStruct((16, 256, 256), BF16),
            jax.ShapeDtypeStruct((NZ, NH, NK, 8, 4096), BF16),
        ),
        in_specs=[smem, smem, vmem, vmem, hbm, hbm, hbm, hbm, hbm],
        out_specs=(hbm, hbm),
        scratch_shapes=[
            pltpu.VMEM((512, 16, 256), BF16),
            pltpu.VMEM((16, 512, 256), BF16),
            pltpu.VMEM((CH, 2, NZ, NH, NK, 16, 256), BF16),
            pltpu.VMEM((16, 64, 512), BF16),
            pltpu.VMEM((2, 2, 256, 256), BF16),
            pltpu.VMEM((CH, 32, 32, 256), BF16),
            pltpu.VMEM((CH, 4, 256, 256), BF16),
            pltpu.VMEM((CH, 4, 256, 256), BF16),
            pltpu.VMEM((CH, 32, 32, 256), BF16),
            pltpu.VMEM((2, LAGS, 256), F32),
            pltpu.VMEM((2, LAGS, 256), BF16),
            pltpu.VMEM((16, LAG_HALF, 128), F32),
            pltpu.VMEM((16, 256, 256), BF16),
            pltpu.VMEM((NZ, NH, NK, 8, 4096), BF16),
            pltpu.VMEM((LAGS, 256), BF16),
            pltpu.VMEM((256, LAGS), BF16),
            pltpu.VMEM((256, 256), BF16),
            pltpu.VMEM((128, 512), BF16),
            dma((12,)),
            dma((3, CH + 1)),
        ]
        + gather_sems
        + [dma((CH + 3,))] * 2
        + [dma((CH + 3,))] * 2
        + [dma((CH + 3,))] * 2
        + [dma((2 * CH,))] * 4,
        compiler_params=pltpu.CompilerParams(
            collective_id=0, has_side_effects=True, vmem_limit_bytes=56 << 20
        ),
        name="c3_exchange",
    )(
        virtual_sources,
        references,
        coda_start.reshape(1, sources),
        coda_end.reshape(1, sources),
        jnp.asarray(inverse),
        jnp.asarray(forward),
        jnp.asarray(swap),
        jnp.asarray(piece),
        spectra.reshape(2 * windows, freq_dev, rcv_dev),
    )
    picked = picked.reshape(picks, 4096)
    steps = freq_dev // FINAL_BINS
    lane_block = lambda c: pl.BlockSpec(
        (256, 64 * FINAL_BINS), lambda n: (0, c * steps + n)
    )
    return pl.pallas_call(
        functools.partial(final_kernel, 1.0 / math.sqrt(sources)),
        grid=(steps,),
        out_shape=jax.ShapeDtypeStruct((2, freq_dev, picks, rcv_dev), F32),
        in_specs=[lane_block(c) for c in range(CH)]
        + [pl.BlockSpec((FINAL_BINS, 256, 256), lambda n: (n, 0, 0))],
        out_specs=pl.BlockSpec((2, FINAL_BINS, 256, 256), lambda n: (0, n, 0, 0)),
        compiler_params=pltpu.CompilerParams(vmem_limit_bytes=60 << 20),
        name="recorrelate",
    )(picked, picked, picked, picked, rel)


def solution(mesh):
    return jax.shard_map(
        per_device,
        mesh=mesh,
        in_specs=(P(None, None, "frq", "rcv"), P(), P(), P(), P()),
        out_specs=P(None, "frq", None, "rcv"),
        check_vma=False,
    )
```
